128 devices in a mesh: ocx: 8 (over x, core), ocy: 16 (over y, z).
Axes of the slice: x: 4, y: 4, z: 4, core: 2. Of those that a mesh axis runs over, the one named last changes fastest.
Arguments:
- ocean_state: float32 [4, 16, 64, 2048], P(None, None, 'ocx', 'ocy'), may hold values from -6 to 6
- floe_state: float32 [4, 65536], P(None, ('ocx', 'ocy')), may hold values from -6 to 6
- floe_props: float32 [2, 65536], P(None, ('ocx', 'ocy')), may hold values from 0.6 to 1.6
- contact_pairs: int32 [2, 512, 512], P(None, ('ocx', 'ocy')), may hold values from 0 to 127, as said below
- bond_ends: int32 [2, 512, 256], P(None, ('ocx', 'ocy')), may hold values from 0 to 127
- bond_broken: int32 [512, 256], P(('ocx', 'ocy')), may hold values 0 or 1
- couple_floe: int32 [128, 9, 128], P(('ocx', 'ocy')), may hold values from 0 to 511, as said below
- couple_weight: float32 [128, 9, 128], P(('ocx', 'ocy')), may hold values from 0 to 1, as said below
- couple_cell: int32 [128, 9, 128], P(('ocx', 'ocy')), may hold values from 0 to 1023, as said below
Outputs:
- ocean_next: float32 [4, 16, 64, 2048], P(None, None, 'ocx', 'ocy')
- floe_next: float32 [4, 65536], P(None, ('ocx', 'ocy'))
The draws below stay inside these ranges and needn't reach their ends.
Inputs may be any that keep to these rules, and one draw needn't show every extreme that they name: `contact_pairs`: unused slots name one floe twice; live slots name two different floes; a tile has at most 512 live slots and some tiles of every draw have 512. `couple_floe`: every slot, used or not, names a floe of its source device. `couple_weight`: zero exactly on unused slots and positive on used ones; in each bucket the used slots come first; buckets toward blocks outside the ocean are empty; every source device has one bucket with all 128 slots used. `couple_cell`: every slot, used or not, names a surface cell of the ocean block.
All inputs are finite; a program needn't handle non-finite values. No bound on the sum of `bond_broken` on one device may be relied on, other than what follows from the above.
Results may differ from the reference program's by a relative error of at most 0.000065.
Values sent between devices are 32-bit elements; how exact they have to be, the bound alone decides.
No kernel may reach another device: no remote copies, remote signals or barrier semaphores. Data moves between devices by JAX's collectives and lax.ppermute only.
A program may use at most 64 MiB of HBM per device.

```python
import math
import jax
import jax.numpy as jnp

CX = 8
CY = 128
LEV = 16
TILE = 128
PAIRS = 512
BONDS = 256
SUBSTEPS = 4
SLOTS = 128
FLOES_DEV = 512
TILES = 512
FLOES = 65536
NX = 64
NY = 2048
N_OCX = 8
N_OCY = 16
DEVICES = 128


def bucket_counts(key):
    sub_key = jax.random.fold_in(key, 4242)
    key_side, key_centre, key_pick = jax.random.split(sub_key, 3)
    device_ids = jnp.arange(DEVICES, dtype=jnp.int32)
    block_row = device_ids // N_OCY
    block_col = device_ids % N_OCY
    near_ids = jnp.arange(9, dtype=jnp.int32)
    target_row = block_row[:, None] + (near_ids // 3 - 1)[None, :]
    target_col = block_col[:, None] + (near_ids % 3 - 1)[None, :]
    inside = (target_row >= 0) & (target_row < N_OCX) & (target_col >= 0) & (target_col < N_OCY)
    side_count = jax.random.randint(key_side, (DEVICES, 9), SLOTS // 8, SLOTS // 2 + 1)
    centre_count = jax.random.randint(key_centre, (DEVICES,), SLOTS // 2, SLOTS + 1)
    counts = side_count.at[:, 4].set(centre_count)
    scores = jax.random.randint(key_pick, (DEVICES, 9), 0, 1000) * 16 + near_ids[None, :]
    scores = jnp.where(inside, scores, -1)
    full_pick = jnp.argmax(scores, axis=1)
    counts = jnp.where(near_ids[None, :] == full_pick[:, None], SLOTS, counts)
    return jnp.where(inside, counts, 0).astype(jnp.int32)


def draw_couple_floe(key, part):
    return jax.random.randint(jax.random.fold_in(key, 101), (DEVICES, 9, SLOTS), 0, FLOES_DEV).astype(jnp.int32)


def draw_couple_cell(key, part):
    return jax.random.randint(jax.random.fold_in(key, 303), (DEVICES, 9, SLOTS), 0, CX * CY).astype(jnp.int32)


def draw_couple_weight(key, part):
    counts = bucket_counts(key)
    slot_index = jnp.arange(SLOTS, dtype=jnp.int32)[None, None, :]
    live_mask = (slot_index < counts[:, :, None]).astype(jnp.float32)
    value_key = jax.random.fold_in(key, 202)
    values = jax.random.uniform(value_key, (DEVICES, 9, SLOTS), jnp.float32, 0.2, 1.0)
    return values * live_mask


def draw_contact_pairs(key, part):
    sub_key = jax.random.fold_in(key, 505)
    key_count, key_hot, key_first, key_step = jax.random.split(sub_key, 4)
    base_count = jax.random.randint(key_count, (TILES,), PAIRS // 6, PAIRS // 2 + 1)
    shuffled = jax.random.permutation(key_hot, TILES)
    hot_mask = jnp.zeros((TILES,), jnp.int32).at[shuffled[:max(1, TILES // 16)]].set(1)
    counts = jnp.where(hot_mask == 1, PAIRS, base_count)
    first_floe = jax.random.randint(key_first, (TILES, PAIRS), 0, TILE)
    stride = jax.random.randint(key_step, (TILES, PAIRS), 1, TILE)
    second = (first_floe + stride) % TILE
    slot_index = jnp.arange(PAIRS, dtype=jnp.int32)[None, :]
    second = jnp.where(slot_index < counts[:, None], second, first_floe)
    return jnp.stack([first_floe, second]).astype(jnp.int32)


def set_ends(array, key, least, high):
    dims = array.shape
    spot = [jax.random.randint(jax.random.fold_in(key, axis), (), 0, dims[axis]) for axis in range(len(dims))]
    array = array.at[tuple(spot)].set(least)
    longest = dims.index(max(dims))
    spot[longest] = (spot[longest] + 1) % dims[longest]
    return array.at[tuple(spot)].set(high)


def block_levels(rng, dims, cuts, smallest, top_value):
    def one(axis_at, parts):
        draws = jax.random.uniform(jax.random.fold_in(jax.random.fold_in(rng, 6), axis_at), (parts,), jnp.float32, smallest / len(cuts), top_value / len(cuts))
        return jnp.repeat(jnp.exp(draws), dims[axis_at] // parts).reshape((-1,) + (1,) * (len(dims) - axis_at - 1))

    level = one(*cuts[0])
    for cut in cuts[1:]:
        level = level * one(*cut)
    return level


def normal_values(stream_key, extent, scale, bound, cuts=(), kind=jnp.bfloat16):
    entries = scale * jax.random.normal(stream_key, extent, jnp.float32)
    if cuts:
        entries = entries * block_levels(stream_key, extent, cuts, -0.22, 0.18)
    return jnp.clip(entries, -bound, bound).astype(kind)


def setup_inputs(seed: int = 0) -> dict:
    splits = jax.random.split(jax.random.key(seed), 10)
    ocean_state = normal_values(splits[0], (4, LEV, NX, NY), 1.0, 6.0, ((2, 8), (3, 16)), jnp.float32)
    floe_state = normal_values(splits[1], (4, FLOES), 1.0, 6.0, ((1, 128),), jnp.float32)
    floe_props = jnp.clip(jnp.exp(math.log(1.6) - 0.98082923 * jax.random.uniform(splits[2], (2, FLOES), jnp.float32) ** block_levels(splits[2], (2, FLOES), ((1, 128),), -0.2, 0.2)), 0.6, 1.6)
    contact_pairs = draw_contact_pairs(jax.random.fold_in(splits[9], 71), 0)
    bond_ends = set_ends(jax.random.randint(splits[4], (2, TILES, BONDS), 0, TILE), jax.random.fold_in(splits[4], 1), 0, TILE - 1).astype(jnp.int32)
    bond_broken = set_ends((jax.random.randint(splits[5], (TILES, BONDS), 0, 4) < 1).astype(jnp.int32), jax.random.fold_in(splits[5], 1), 0, 1)
    couple_floe = draw_couple_floe(jax.random.fold_in(splits[9], 71), 0)
    couple_weight = draw_couple_weight(jax.random.fold_in(splits[9], 71), 0)
    couple_cell = draw_couple_cell(jax.random.fold_in(splits[9], 71), 0)
    return {"ocean_state": ocean_state, "floe_state": floe_state, "floe_props": floe_props, "contact_pairs": contact_pairs, "bond_ends": bond_ends, "bond_broken": bond_broken, "couple_floe": couple_floe, "couple_weight": couple_weight, "couple_cell": couple_cell}


TIME_STEP = 0.05
CONTACT_STIFF = 2.0
CONTACT_DAMP = 0.2
BOND_DAMP = 0.3
DRAG_COEF = 0.5
HEAT_COEF = 0.3
SALT_COEF = 0.2
FREEZE = -1.8
DIFFUSE_SIDE = 0.15
DIFFUSE_DEPTH = 0.2
CORIOLIS = 0.3
PRESSURE_COEF = 0.1
THERMAL_EXP = 0.2
HALINE_CONTR = 0.8


def ocean_update(padded, forcing):
    interior = padded[:, :, 1:-1, 1:-1]
    laplace_side = padded[:, :, 2:, 1:-1] + padded[:, :, :-2, 1:-1] + padded[:, :, 1:-1, 2:] + padded[:, :, 1:-1, :-2] - 4.0 * interior
    above_cells = jnp.concatenate([interior[:, :1], interior[:, :-1]], axis=1)
    below_cells = jnp.concatenate([interior[:, 1:], interior[:, -1:]], axis=1)
    laplace_depth = above_cells + below_cells - 2.0 * interior
    density = HALINE_CONTR * padded[3] - THERMAL_EXP * padded[2]
    pressure = jnp.cumsum(density, axis=0)
    grad_x = 0.5 * (pressure[:, 2:, 1:-1] - pressure[:, :-2, 1:-1])
    grad_y = 0.5 * (pressure[:, 1:-1, 2:] - pressure[:, 1:-1, :-2])
    east_vel = interior[0]
    north_vel = interior[1]
    tendency = DIFFUSE_SIDE * laplace_side + DIFFUSE_DEPTH * laplace_depth
    momentum = jnp.stack([CORIOLIS * north_vel - PRESSURE_COEF * grad_x, -CORIOLIS * east_vel - PRESSURE_COEF * grad_y])
    tendency = tendency.at[:2].add(momentum)
    tendency = tendency.at[:, 0].add(forcing)
    return interior + tendency


def floe_steps(floe_state, floe_props, contact_pairs, bond_ends, bond_broken, intersection_area, drag_sum):
    floe_count = floe_state.shape[1]
    tile_count = floe_count // TILE
    radius = floe_props[0]
    inv_mass = 1.0 / (floe_props[1] * radius * radius)
    offset = (jnp.arange(tile_count, dtype=jnp.int32) * TILE)[:, None]
    first_floe = (contact_pairs[0] + offset).reshape(-1)
    second = (contact_pairs[1] + offset).reshape(-1)
    bond_first = (bond_ends[0] + offset).reshape(-1)
    bond_second = (bond_ends[1] + offset).reshape(-1)
    bond_alive = (1 - bond_broken).astype(jnp.float32).reshape(-1)
    reach_sq = (radius[first_floe] + radius[second]) ** 2
    positions = floe_state[:2]
    velocity = floe_state[2:]
    mean_vel = jnp.zeros_like(velocity)
    for substep in range(SUBSTEPS):
        separation = positions[:, second] - positions[:, first_floe]
        contact_depth = jnp.maximum(1.0 - (separation[0] ** 2 + separation[1] ** 2) / reach_sq, 0.0)
        relative = velocity[:, second] - velocity[:, first_floe]
        pair_force = contact_depth * (CONTACT_DAMP * relative - CONTACT_STIFF * separation)
        bond_force = BOND_DAMP * bond_alive * (velocity[:, bond_second] - velocity[:, bond_first])
        total_force = DRAG_COEF * (drag_sum - intersection_area * velocity)
        total_force = total_force.at[:, first_floe].add(pair_force).at[:, second].add(-pair_force)
        total_force = total_force.at[:, bond_first].add(bond_force).at[:, bond_second].add(-bond_force)
        velocity = velocity + TIME_STEP * inv_mass * total_force
        positions = positions + TIME_STEP * velocity
        mean_vel = mean_vel + velocity / SUBSTEPS
    return jnp.concatenate([positions, velocity], axis=0), mean_vel


def floe_side(floe_state, floe_props, contact_pairs, bond_ends, bond_broken, floe_index, weight, samples):
    floe_count = floe_state.shape[1]
    intersection_area = jnp.zeros((floe_count,), jnp.float32).at[floe_index].add(weight)
    drag_sum = jnp.zeros((2, floe_count), jnp.float32).at[:, floe_index].add(weight * samples[:2])
    floe_next, mean_vel = floe_steps(floe_state, floe_props, contact_pairs, bond_ends, bond_broken, intersection_area, drag_sum)
    ice_vel = mean_vel[:, floe_index]
    stress = DRAG_COEF * weight * (ice_vel - samples[:2])
    heat_flux = HEAT_COEF * weight * (FREEZE - samples[2])
    salt_flux = SALT_COEF * weight * floe_props[1][floe_index]
    return floe_next, jnp.concatenate([stress, heat_flux[None], salt_flux[None]], axis=0)


def reference(ocean_state, floe_state, floe_props, contact_pairs, bond_ends, bond_broken, couple_floe, couple_weight, couple_cell):
    cell_count = CX * CY
    surface = ocean_state[:, 0]
    blocks = surface.reshape(4, N_OCX, CX, N_OCY, CY).transpose(0, 1, 3, 2, 4).reshape(4, DEVICES * cell_count)
    device_ids = jnp.arange(DEVICES, dtype=jnp.int32)
    block_row = device_ids // N_OCY
    block_col = device_ids % N_OCY
    near_ids = jnp.arange(9, dtype=jnp.int32)
    step_x = near_ids // 3 - 1
    step_y = near_ids % 3 - 1
    target_row = block_row[:, None] + step_x[None, :]
    target_col = block_col[:, None] + step_y[None, :]
    inside = (target_row >= 0) & (target_row < N_OCX) & (target_col >= 0) & (target_col < N_OCY)
    target = (jnp.clip(target_row, 0, N_OCX - 1) * N_OCY + jnp.clip(target_col, 0, N_OCY - 1)).astype(jnp.int32)
    back_ids = (8 - near_ids)[None, :]
    cell_at = couple_cell[target, back_ids]
    cell_flat = (target[:, :, None] * cell_count + cell_at).astype(jnp.int32).reshape(-1)
    inside_flat = jnp.broadcast_to(inside[:, :, None], (DEVICES, 9, SLOTS)).astype(jnp.float32).reshape(-1)
    sampled = blocks[:, cell_flat] * inside_flat
    floe_index = (couple_floe + device_ids[:, None, None] * FLOES_DEV).astype(jnp.int32).reshape(-1)
    weight = couple_weight.reshape(-1)
    floe_next, flux = floe_side(floe_state, floe_props, contact_pairs, bond_ends, bond_broken, floe_index, weight, sampled)
    forcing = jnp.zeros((4, DEVICES * cell_count), jnp.float32).at[:, cell_flat].add(flux * inside_flat)
    forcing_grid = forcing.reshape(4, N_OCX, N_OCY, CX, CY).transpose(0, 1, 3, 2, 4).reshape(4, NX, NY)
    padded = jnp.pad(ocean_state, ((0, 0), (0, 0), (1, 1), (1, 1)))
    return ocean_update(padded, forcing_grid), floe_next
```

```python
import jax
import jax.numpy as jnp
from jax import lax
from jax.experimental import pallas as pl
from jax.experimental.pallas import tpu as pltpu
from jax.sharding import PartitionSpec as P

F32 = jnp.float32
BF16 = jnp.bfloat16
I32 = jnp.int32

TILE = 128
TILES = 4
SUBSTEPS = 4
LEV = 16
BUCKETS = 9
ENTRIES = BUCKETS * 128
TIME_STEP = 0.05
CONTACT_STIFF = 2.0
CONTACT_DAMP = 0.2
BOND_DAMP = 0.3
DRAG_COEF = 0.5
HEAT_COEF = 0.3
SALT_COEF = 0.2
FREEZE = -1.8
DIFFUSE_SIDE = 0.15
DIFFUSE_DEPTH = 0.2
CORIOLIS = 0.3
PRESSURE_COEF = 0.1
THERMAL_EXP = 0.2
HALINE_CONTR = 0.8
AXES = ("ocx", "ocy")
VMEM_SPEC = pl.BlockSpec(memory_space=pltpu.VMEM)


def call(kernel, outs, *args, cost=0):
    return pl.pallas_call(
        kernel,
        out_shape=outs,
        in_specs=[VMEM_SPEC] * len(args),
        out_specs=jax.tree.map(lambda _: VMEM_SPEC, outs),
        cost_estimate=pl.CostEstimate(flops=cost, bytes_accessed=1 << 16, transcendentals=0),
    )(*args)


def shaped(*shape, dtype=F32):
    return jax.ShapeDtypeStruct(shape, dtype)


def split3(x):
    hi = x.astype(BF16).astype(F32)
    rest = x - hi
    mid = rest.astype(BF16).astype(F32)
    return jnp.concatenate([hi, mid, rest - mid], axis=0).astype(BF16)


def join3(y):
    n = y.shape[0] // 3
    return y[:n] + y[n : 2 * n] + y[2 * n :]


def dot_nn(a, b):
    return lax.dot_general(a, b, (((1,), (0,)), ((), ())), preferred_element_type=F32)


def dot_nt(a, b):
    return lax.dot_general(a, b, (((1,), (1,)), ((), ())), preferred_element_type=F32)


def lanes_row(ref):
    return jnp.concatenate([ref[m] for m in range(BUCKETS)], axis=1)


def one_hot(row):
    n = row.shape[1]
    ids = lax.broadcasted_iota(I32, (128, n), 0)
    return jnp.where(ids == jnp.broadcast_to(row, (128, n)), 1.0, 0.0).astype(BF16)


def is_even(axis):
    return lax.rem(lax.axis_index(axis), 2) == 0


def send_both(even, toward_plus, toward_minus, even_ref, odd_ref, row, rows):
    even_ref[pl.ds(row, rows), :] = jnp.where(even, toward_plus, toward_minus)
    odd_ref[pl.ds(row, rows), :] = jnp.where(even, toward_minus, toward_plus)


def bucket_rows(fields, a):
    rows = [f[:, (3 * a + b) * 128 : (3 * a + b + 1) * 128] for f in fields for b in range(3)]
    return jnp.concatenate(rows, axis=0)


def sample_kernel(ocean_ref, cell_ref, even_ref, odd_ref, own_ref):
    even = is_even("ocx")
    cells = lanes_row(cell_ref)
    table = one_hot(cells & 127)
    surface = jnp.concatenate([ocean_ref[pl.ds(f * 128, 8), :] for f in range(3)], axis=0)
    picked = join3(dot_nn(split3(surface), table))
    row_hit = lax.broadcasted_iota(I32, (8, ENTRIES), 0) == jnp.broadcast_to(
        cells >> 7, (8, ENTRIES)
    )
    fields = [
        jnp.sum(jnp.where(row_hit, picked[8 * f : 8 * f + 8], 0.0), axis=0, keepdims=True)
        for f in range(3)
    ]
    send_both(even, bucket_rows(fields, 2), bucket_rows(fields, 0), even_ref, odd_ref, 0, 9)
    own_ref[pl.ds(0, 9), :] = bucket_rows(fields, 1)
    first = ocean_ref[pl.ds(0, 64, stride=8), :]
    last = ocean_ref[pl.ds(7, 64, stride=8), :]
    send_both(even, last, first, even_ref, odd_ref, 16, 64)


def column_kernel(ocean_ref, floe_ref, weight_ref, props_ref, cols_ref, table_ref, area_ref, salt_ref):
    for f in range(4):
        turned = ocean_ref[pl.ds(f * 128, 128), :].T
        cols_ref[pl.ds(f, 1), :] = turned[127:128]
        cols_ref[pl.ds(4 + f, 1), :] = turned[0:1]
    floes = lanes_row(floe_ref)
    weight = lanes_row(weight_ref)
    table = one_hot(floes & 127)
    table_ref[...] = table
    tile_hit = (lax.broadcasted_iota(I32, (8, ENTRIES), 0) & 3) == jnp.broadcast_to(
        floes >> 7, (8, ENTRIES)
    )
    spread = jnp.where(tile_hit, jnp.broadcast_to(weight, (8, ENTRIES)), 0.0)
    area_ref[...] = join3(dot_nt(split3(spread), table))
    thick = jnp.concatenate(
        [props_ref[pl.ds(1, 1), pl.ds(t * 128, 128)] for t in range(TILES)] * 2, axis=0
    )
    picked = join3(dot_nn(split3(thick), table))
    chosen = jnp.sum(jnp.where(tile_hit, picked, 0.0)[:4], axis=0, keepdims=True)
    salt_ref[...] = SALT_COEF * weight * chosen


def tile_rows(ref, k):
    return jnp.concatenate(
        [ref[pl.ds(k, 1), pl.ds(t * 128, 128)] for t in range(TILES)], axis=0
    )


def pair_forces(x8, v8, reach_ref, contact_ref, bond_ref):
    turned = jnp.concatenate([x8, v8], axis=0).T
    rows = [[None] * TILES for _ in range(2)]
    step = 32

    def column(c, lo):
        return jnp.broadcast_to(turned[lo : lo + step, c : c + 1], (step, 128))

    def wide(row):
        return jnp.broadcast_to(row, (step, 128))

    for t in range(TILES):
        total_x = jnp.zeros((8, 128), F32)
        total_y = jnp.zeros((8, 128), F32)
        for lo in range(0, 128, step):
            part = pl.ds(lo, step)
            dx = column(t, lo) - wide(x8[t : t + 1])
            dy = column(4 + t, lo) - wide(x8[4 + t : 5 + t])
            depth = jnp.maximum(1.0 - (dx * dx + dy * dy) * reach_ref[t, part, :], 0.0)
            stiff = depth * contact_ref[t, part, :]
            damp = (CONTACT_DAMP / CONTACT_STIFF) * stiff + bond_ref[t, part, :]
            dvx = column(8 + t, lo) - wide(v8[t : t + 1])
            dvy = column(12 + t, lo) - wide(v8[4 + t : 5 + t])
            fx = damp * dvx - stiff * dx
            fy = damp * dvy - stiff * dy
            total_x = total_x + jnp.sum(fx.reshape(step // 8, 8, 128), axis=0)
            total_y = total_y + jnp.sum(fy.reshape(step // 8, 8, 128), axis=0)
        rows[0][t] = jnp.sum(total_x, axis=0, keepdims=True)
        rows[1][t] = jnp.sum(total_y, axis=0, keepdims=True)
    return jnp.concatenate(rows[0] + rows[1], axis=0)


def state_rows(state_ref):
    x8 = jnp.concatenate([tile_rows(state_ref, 0), tile_rows(state_ref, 1)], axis=0)
    v8 = jnp.concatenate([tile_rows(state_ref, 2), tile_rows(state_ref, 3)], axis=0)
    return x8, v8


def pair_kernel(
    pairs_ref, bonds_ref, broken_ref, props_ref, state_ref, reach_ref, contact_ref, bond_ref, force_ref
):
    def differences(ref, t, n):
        ids = lax.broadcasted_iota(I32, (128, n), 0)
        first = jnp.broadcast_to(ref[0, pl.ds(t, 1), :], (128, n))
        second = jnp.broadcast_to(ref[1, pl.ds(t, 1), :], (128, n))
        return jnp.where(ids == second, 1.0, 0.0) - jnp.where(ids == first, 1.0, 0.0)

    radius = tile_rows(props_ref, 0)
    radius_columns = jnp.concatenate([radius, radius], axis=0).T
    for t in range(TILES):
        slots = differences(pairs_ref, t, 512).astype(BF16)
        contact_ref[t] = -CONTACT_STIFF * dot_nt(slots, slots)
        alive = jnp.broadcast_to(broken_ref[pl.ds(t, 1), :], (128, 256)) == 0
        ends = jnp.where(alive, differences(bonds_ref, t, 256), 0.0).astype(BF16)
        bond_ref[t] = -BOND_DAMP * dot_nt(ends, ends)
        reach = jnp.broadcast_to(radius_columns[:, t : t + 1], (128, 128)) + jnp.broadcast_to(
            radius[t : t + 1], (128, 128)
        )
        reach_ref[t] = 1.0 / (reach * reach)
    x8, v8 = state_rows(state_ref)
    force_ref[...] = pair_forces(x8, v8, reach_ref, contact_ref, bond_ref)


def from_sides(even, got_even, got_odd):
    return jnp.where(even, got_odd, got_even), jnp.where(even, got_even, got_odd)


def turn_rows(low, own, high, count):
    return [
        jnp.concatenate(
            [src[3 * f + b : 3 * f + b + 1] for f in range(count) for src in (low, own, high)],
            axis=0,
        )
        for b in range(3)
    ]


def turn_kernel(count, with_cols):
    def kernel(*refs):
        if with_cols:
            got_even_ref, got_odd_ref, own_ref, cols_ref, even_ref, odd_ref, keep_ref = refs
        else:
            got_even_ref, got_odd_ref, own_ref, even_ref, odd_ref, keep_ref = refs
        part = pl.ds(0, 3 * count)
        low, high = from_sides(is_even("ocx"), got_even_ref[part, :], got_odd_ref[part, :])
        down, keep, up = turn_rows(low, own_ref[part, :], high, count)
        even = is_even("ocy")
        send_both(even, up, down, even_ref, odd_ref, 0, 3 * count)
        if with_cols:
            send_both(even, cols_ref[0:4], cols_ref[4:8], even_ref, odd_ref, 12, 4)
        keep_ref[part, :] = keep

    return kernel


def entry_rows(got_even_ref, got_odd_ref, keep_ref, count):
    part = pl.ds(0, 3 * count)
    low, high = from_sides(is_even("ocy"), got_even_ref[part, :], got_odd_ref[part, :])
    keep = keep_ref[part, :]
    return [
        jnp.concatenate(
            [src[3 * f + a : 3 * f + a + 1] for a in range(3) for src in (low, keep, high)], axis=1
        )
        for f in range(count)
    ]


def floe_kernel(
    got_even_ref,
    got_odd_ref,
    keep_ref,
    floe_ref,
    weight_ref,
    table_ref,
    area_ref,
    salt_ref,
    reach_ref,
    contact_ref,
    bond_ref,
    force_ref,
    state_ref,
    props_ref,
    next_ref,
    even_ref,
    odd_ref,
    own_ref,
):
    samples = entry_rows(got_even_ref, got_odd_ref, keep_ref, 3)
    weight = lanes_row(weight_ref)
    floes = lanes_row(floe_ref)
    table = table_ref[...]
    ids = lax.broadcasted_iota(I32, (8, ENTRIES), 0)
    tile_hit = (ids & 3) == jnp.broadcast_to(floes >> 7, (8, ENTRIES))
    wide = jnp.where(
        ids < 4,
        jnp.broadcast_to(weight * samples[0], (8, ENTRIES)),
        jnp.broadcast_to(weight * samples[1], (8, ENTRIES)),
    )
    drag = join3(dot_nt(split3(jnp.where(tile_hit, wide, 0.0)), table))
    area = area_ref[...]
    radius = tile_rows(props_ref, 0)
    inv_mass = 1.0 / (tile_rows(props_ref, 1) * radius * radius)
    push = TIME_STEP * jnp.concatenate([inv_mass, inv_mass], axis=0)
    x8, v8 = state_rows(state_ref)
    mean = jnp.zeros((8, 128), F32)
    for substep in range(SUBSTEPS):
        if substep == 0:
            force = force_ref[...]
        else:
            force = pair_forces(x8, v8, reach_ref, contact_ref, bond_ref)
        force = force + DRAG_COEF * (drag - area * v8)
        v8 = v8 + push * force
        x8 = x8 + TIME_STEP * v8
        mean = mean + v8 * (1.0 / SUBSTEPS)
    for k in range(2):
        for t in range(TILES):
            lanes = pl.ds(t * 128, 128)
            next_ref[pl.ds(k, 1), lanes] = x8[4 * k + t : 4 * k + t + 1]
            next_ref[pl.ds(2 + k, 1), lanes] = v8[4 * k + t : 4 * k + t + 1]
    picked = jnp.where(tile_hit, join3(dot_nn(split3(mean), table)), 0.0)
    flux = [
        DRAG_COEF
        * weight
        * (jnp.sum(picked[4 * k : 4 * k + 4], axis=0, keepdims=True) - samples[k])
        for k in range(2)
    ]
    flux = flux + [HEAT_COEF * weight * (FREEZE - samples[2]), salt_ref[...]]
    send_both(
        is_even("ocx"), bucket_rows(flux, 2), bucket_rows(flux, 0), even_ref, odd_ref, 0, 12
    )
    own_ref[pl.ds(0, 12), :] = bucket_rows(flux, 1)


def ocean_kernel(ocean_ref, x_even_ref, x_odd_ref, y_even_ref, y_odd_ref, out_ref, low_ref, high_ref):
    i, j = lax.axis_index("ocx"), lax.axis_index("ocy")
    x_even, y_even = lax.rem(i, 2) == 0, lax.rem(j, 2) == 0
    rows = pl.ds(16, 64)
    low, high = from_sides(x_even, x_even_ref[rows, :], x_odd_ref[rows, :])
    low_ref[...] = jnp.where(i == 0, 0.0, low)
    high_ref[...] = jnp.where(i == lax.axis_size("ocx") - 1, 0.0, high)
    rows = pl.ds(12, 4)
    left, right = from_sides(y_even, y_even_ref[rows, :], y_odd_ref[rows, :])
    left = jnp.where(j == 0, 0.0, left)
    right = jnp.where(j == lax.axis_size("ocy") - 1, 0.0, right)
    turned = jnp.concatenate([left, right], axis=0).T
    sub = lax.broadcasted_iota(I32, (8, 128), 0)
    lane = lax.broadcasted_iota(I32, (8, 128), 1)
    at_low, at_high = sub == 0, sub == 7
    at_left, at_right = lane == 0, lane == 127

    def block(f, l):
        return ocean_ref[pl.ds((f * LEV + l) * 8, 8), :]

    def neighbours(f, l, here):
        k = f * LEV + l
        below = jnp.where(
            at_low, jnp.broadcast_to(low_ref[pl.ds(k, 1), :], (8, 128)), pltpu.roll(here, 1, 0)
        )
        above = jnp.where(
            at_high, jnp.broadcast_to(high_ref[pl.ds(k, 1), :], (8, 128)), pltpu.roll(here, 7, 0)
        )
        edge = turned[l * 8 : l * 8 + 8]
        left = jnp.where(
            at_left, jnp.broadcast_to(edge[:, f : f + 1], (8, 128)), pltpu.roll(here, 1, 1)
        )
        right = jnp.where(
            at_right, jnp.broadcast_to(edge[:, 4 + f : 5 + f], (8, 128)), pltpu.roll(here, 127, 1)
        )
        return below, above, left, right

    grad_x = jnp.zeros((8, 128), F32)
    grad_y = jnp.zeros((8, 128), F32)
    for l in range(LEV):
        here = [block(f, l) for f in range(4)]
        around = [neighbours(f, l, here[f]) for f in range(4)]
        below, above, left, right = zip(*around)
        grad_x = grad_x + (
            (0.5 * HALINE_CONTR) * (above[3] - below[3]) - (0.5 * THERMAL_EXP) * (above[2] - below[2])
        )
        grad_y = grad_y + (
            (0.5 * HALINE_CONTR) * (right[3] - left[3]) - (0.5 * THERMAL_EXP) * (right[2] - left[2])
        )
        for f in range(4):
            side = below[f] + above[f] + left[f] + right[f] - 4.0 * here[f]
            depth = block(f, max(l - 1, 0)) + block(f, min(l + 1, LEV - 1)) - 2.0 * here[f]
            new = here[f] + DIFFUSE_SIDE * side + DIFFUSE_DEPTH * depth
            if f == 0:
                new = new + CORIOLIS * here[1] - PRESSURE_COEF * grad_x
            if f == 1:
                new = new - CORIOLIS * here[0] - PRESSURE_COEF * grad_y
            out_ref[pl.ds((f * LEV + l) * 8, 8), :] = new


def forcing_kernel(got_even_ref, got_odd_ref, keep_ref, cell_ref, ocean_ref, out_ref):
    cells = lanes_row(cell_ref)
    table = one_hot(cells & 127)
    row_hit = lax.broadcasted_iota(I32, (8, ENTRIES), 0) == jnp.broadcast_to(
        cells >> 7, (8, ENTRIES)
    )
    flux = entry_rows(got_even_ref, got_odd_ref, keep_ref, 4)
    spread = jnp.concatenate(
        [jnp.where(row_hit, jnp.broadcast_to(row, (8, ENTRIES)), 0.0) for row in flux], axis=0
    )
    forcing = join3(dot_nt(split3(spread), table))
    out_ref[...] = ocean_ref[...]
    for f in range(4):
        rows = pl.ds(f * LEV * 8, 8)
        out_ref[rows, :] = ocean_ref[rows, :] + forcing[8 * f : 8 * f + 8]


def pairings(nx, ny):
    def both(pair_of):
        return [(i * ny + j, pair_of(i, j)) for i in range(nx) for j in range(ny)]

    def odd_x(i, j):
        if i in (0, nx - 1):
            return i * ny + (j ^ 1)
        return (i + 1 if i % 2 else i - 1) * ny + j

    def odd_y(i, j):
        if j in (0, ny - 1):
            return (i ^ 1) * ny + j
        return i * ny + (j + 1 if j % 2 else j - 1)

    return (
        both(lambda i, j: (i ^ 1) * ny + j),
        both(odd_x),
        both(lambda i, j: i * ny + (j ^ 1)),
        both(odd_y),
    )


def shards(nx, ny):
    x_even, x_odd, y_even, y_odd = pairings(nx, ny)

    def body(
        ocean_state,
        floe_state,
        floe_props,
        contact_pairs,
        bond_ends,
        bond_broken,
        couple_floe,
        couple_weight,
        couple_cell,
    ):
        ocean = ocean_state.reshape(4 * LEV * 8, 128)
        floe = couple_floe.reshape(BUCKETS, 1, 128)
        weight = couple_weight.reshape(BUCKETS, 1, 128)
        cell = couple_cell.reshape(BUCKETS, 1, 128)
        small = shaped(16, 128)
        send_even, send_odd, own = call(
            sample_kernel, (shaped(80, 128), shaped(80, 128), small), ocean, cell
        )
        ge_x = lax.ppermute(send_even, AXES, x_even)
        go_x = lax.ppermute(send_odd, AXES, x_odd)
        cols, table, area, salt = call(
            column_kernel,
            (shaped(8, 128), shaped(128, ENTRIES, dtype=BF16), shaped(8, 128), shaped(1, ENTRIES)),
            ocean,
            floe,
            weight,
            floe_props,
        )
        send_even, send_odd, keep = call(
            turn_kernel(3, True), (small, small, small), ge_x, go_x, own, cols
        )
        ge_y = lax.ppermute(send_even, AXES, y_even)
        go_y = lax.ppermute(send_odd, AXES, y_odd)
        square = shaped(TILES, 128, 128)
        reach, contact, bond, force = call(
            pair_kernel,
            (square, square, square, shaped(8, 128)),
            contact_pairs,
            bond_ends,
            bond_broken,
            floe_props,
            floe_state,
        )
        floe_next, send_even, send_odd, own = call(
            floe_kernel,
            (shaped(4, 512), small, small, small),
            ge_y,
            go_y,
            keep,
            floe,
            weight,
            table,
            area,
            salt,
            reach,
            contact,
            bond,
            force,
            floe_state,
            floe_props,
        )
        he_x = lax.ppermute(send_even, AXES, x_even)
        ho_x = lax.ppermute(send_odd, AXES, x_odd)
        send_even, send_odd, keep = call(
            turn_kernel(4, False), (small, small, small), he_x, ho_x, own
        )
        he_y = lax.ppermute(send_even, AXES, y_even)
        ho_y = lax.ppermute(send_odd, AXES, y_odd)
        moved = pl.pallas_call(
            ocean_kernel,
            out_shape=shaped(4 * LEV * 8, 128),
            in_specs=[VMEM_SPEC] * 5,
            out_specs=VMEM_SPEC,
            scratch_shapes=[pltpu.VMEM((64, 128), F32), pltpu.VMEM((64, 128), F32)],
        )(ocean, ge_x, go_x, ge_y, go_y)
        ocean_next = call(forcing_kernel, shaped(4 * LEV * 8, 128), he_y, ho_y, keep, cell, moved)
        return (ocean_next.reshape(ocean_state.shape), floe_next)

    return body


def solution(mesh):
    in_specs = (
        P(None, None, "ocx", "ocy"),
        P(None, ("ocx", "ocy")),
        P(None, ("ocx", "ocy")),
        P(None, ("ocx", "ocy"), None),
        P(None, ("ocx", "ocy"), None),
        P(("ocx", "ocy"), None),
        P(("ocx", "ocy"), None, None),
        P(("ocx", "ocy"), None, None),
        P(("ocx", "ocy"), None, None),
    )
    out_specs = (P(None, None, "ocx", "ocy"), P(None, ("ocx", "ocy")))
    body = shards(mesh.shape["ocx"], mesh.shape["ocy"])
    return jax.shard_map(body, mesh=mesh, in_specs=in_specs, out_specs=out_specs, check_vma=False)
```

```python
import jax
import jax.numpy as jnp
from jax import lax
from jax.experimental import pallas as pl
from jax.experimental.pallas import tpu as pltpu
from jax.sharding import PartitionSpec as P

F32 = jnp.float32
BF16 = jnp.bfloat16
I32 = jnp.int32

TILE = 128
TILES = 4
SUBSTEPS = 4
LEV = 16
BUCKETS = 9
ENTRIES = BUCKETS * 128
TIME_STEP = 0.05
CONTACT_STIFF = 2.0
CONTACT_DAMP = 0.2
BOND_DAMP = 0.3
DRAG_COEF = 0.5
HEAT_COEF = 0.3
SALT_COEF = 0.2
FREEZE = -1.8
DIFFUSE_SIDE = 0.15
DIFFUSE_DEPTH = 0.2
CORIOLIS = 0.3
PRESSURE_COEF = 0.1
THERMAL_EXP = 0.2
HALINE_CONTR = 0.8
AXES = ("ocx", "ocy")
VMEM_SPEC = pl.BlockSpec(memory_space=pltpu.VMEM)
GRANT = pltpu.CompilerParams(vmem_limit_bytes=8 << 20)


def call(kernel, outs, *args, cost=0):
    return pl.pallas_call(
        kernel,
        out_shape=outs,
        in_specs=[VMEM_SPEC] * len(args),
        out_specs=jax.tree.map(lambda _: VMEM_SPEC, outs),
        cost_estimate=pl.CostEstimate(flops=cost, bytes_accessed=1 << 16, transcendentals=0),
        compiler_params=GRANT,
    )(*args)


def shaped(*shape, dtype=F32):
    return jax.ShapeDtypeStruct(shape, dtype)


def split3(x):
    hi = x.astype(BF16).astype(F32)
    rest = x - hi
    mid = rest.astype(BF16).astype(F32)
    return jnp.concatenate([hi, mid, rest - mid], axis=0).astype(BF16)


def join3(y):
    n = y.shape[0] // 3
    return y[:n] + y[n : 2 * n] + y[2 * n :]


def dot_nn(a, b):
    return lax.dot_general(a, b, (((1,), (0,)), ((), ())), preferred_element_type=F32)


def dot_nt(a, b):
    return lax.dot_general(a, b, (((1,), (1,)), ((), ())), preferred_element_type=F32)


def lanes_row(ref):
    return jnp.concatenate([ref[m] for m in range(BUCKETS)], axis=1)


def one_hot(row):
    n = row.shape[1]
    ids = lax.broadcasted_iota(I32, (128, n), 0)
    return jnp.where(ids == jnp.broadcast_to(row, (128, n)), 1.0, 0.0).astype(BF16)


def is_even(axis):
    return lax.rem(lax.axis_index(axis), 2) == 0


def send_both(even, toward_plus, toward_minus, even_ref, odd_ref, row, rows):
    even_ref[pl.ds(row, rows), :] = jnp.where(even, toward_plus, toward_minus)
    odd_ref[pl.ds(row, rows), :] = jnp.where(even, toward_minus, toward_plus)


def bucket_rows(fields, a):
    rows = [f[:, (3 * a + b) * 128 : (3 * a + b + 1) * 128] for f in fields for b in range(3)]
    return jnp.concatenate(rows, axis=0)


def sample_kernel(ocean_ref, cell_ref, even_ref, odd_ref, own_ref):
    even = is_even("ocx")
    cells = lanes_row(cell_ref)
    table = one_hot(cells & 127)
    surface = jnp.concatenate([ocean_ref[pl.ds(f * 128, 8), :] for f in range(3)], axis=0)
    picked = join3(dot_nn(split3(surface), table))
    row_hit = lax.broadcasted_iota(I32, (8, ENTRIES), 0) == jnp.broadcast_to(
        cells >> 7, (8, ENTRIES)
    )
    fields = [
        jnp.sum(jnp.where(row_hit, picked[8 * f : 8 * f + 8], 0.0), axis=0, keepdims=True)
        for f in range(3)
    ]
    send_both(even, bucket_rows(fields, 2), bucket_rows(fields, 0), even_ref, odd_ref, 0, 9)
    own_ref[pl.ds(0, 9), :] = bucket_rows(fields, 1)
    first = ocean_ref[pl.ds(0, 64, stride=8), :]
    last = ocean_ref[pl.ds(7, 64, stride=8), :]
    send_both(even, last, first, even_ref, odd_ref, 16, 64)


def column_kernel(ocean_ref, floe_ref, weight_ref, props_ref, cols_ref, table_ref, area_ref, salt_ref):
    for f in range(4):
        turned = ocean_ref[pl.ds(f * 128, 128), :].T
        cols_ref[pl.ds(f, 1), :] = turned[127:128]
        cols_ref[pl.ds(4 + f, 1), :] = turned[0:1]
    floes = lanes_row(floe_ref)
    weight = lanes_row(weight_ref)
    table = one_hot(floes & 127)
    table_ref[...] = table
    tile_hit = (lax.broadcasted_iota(I32, (8, ENTRIES), 0) & 3) == jnp.broadcast_to(
        floes >> 7, (8, ENTRIES)
    )
    spread = jnp.where(tile_hit, jnp.broadcast_to(weight, (8, ENTRIES)), 0.0)
    area_ref[...] = join3(dot_nt(split3(spread), table))
    thick = jnp.concatenate(
        [props_ref[pl.ds(1, 1), pl.ds(t * 128, 128)] for t in range(TILES)] * 2, axis=0
    )
    picked = join3(dot_nn(split3(thick), table))
    chosen = jnp.sum(jnp.where(tile_hit, picked, 0.0)[:4], axis=0, keepdims=True)
    salt_ref[...] = SALT_COEF * weight * chosen


def tile_rows(ref, k):
    return jnp.concatenate(
        [ref[pl.ds(k, 1), pl.ds(t * 128, 128)] for t in range(TILES)], axis=0
    )


def pair_forces(x8, v8, reach_ref, contact_ref, bond_ref):
    turned = jnp.concatenate([x8, v8], axis=0).T
    rows = [[None] * TILES for _ in range(2)]
    step = 32

    def column(c, lo):
        return jnp.broadcast_to(turned[lo : lo + step, c : c + 1], (step, 128))

    def wide(row):
        return jnp.broadcast_to(row, (step, 128))

    for t in range(TILES):
        total_x = jnp.zeros((8, 128), F32)
        total_y = jnp.zeros((8, 128), F32)
        for lo in range(0, 128, step):
            part = pl.ds(lo, step)
            dx = column(t, lo) - wide(x8[t : t + 1])
            dy = column(4 + t, lo) - wide(x8[4 + t : 5 + t])
            depth = jnp.maximum(1.0 - (dx * dx + dy * dy) * reach_ref[t, part, :], 0.0)
            stiff = depth * contact_ref[t, part, :]
            damp = (CONTACT_DAMP / CONTACT_STIFF) * stiff + bond_ref[t, part, :]
            dvx = column(8 + t, lo) - wide(v8[t : t + 1])
            dvy = column(12 + t, lo) - wide(v8[4 + t : 5 + t])
            fx = damp * dvx - stiff * dx
            fy = damp * dvy - stiff * dy
            total_x = total_x + jnp.sum(fx.reshape(step // 8, 8, 128), axis=0)
            total_y = total_y + jnp.sum(fy.reshape(step // 8, 8, 128), axis=0)
        rows[0][t] = jnp.sum(total_x, axis=0, keepdims=True)
        rows[1][t] = jnp.sum(total_y, axis=0, keepdims=True)
    return jnp.concatenate(rows[0] + rows[1], axis=0)


def state_rows(state_ref):
    x8 = jnp.concatenate([tile_rows(state_ref, 0), tile_rows(state_ref, 1)], axis=0)
    v8 = jnp.concatenate([tile_rows(state_ref, 2), tile_rows(state_ref, 3)], axis=0)
    return x8, v8


def pair_kernel(
    pairs_ref, bonds_ref, broken_ref, props_ref, state_ref, reach_ref, contact_ref, bond_ref, force_ref
):
    def differences(ref, t, n):
        ids = lax.broadcasted_iota(I32, (128, n), 0)
        first = jnp.broadcast_to(ref[0, pl.ds(t, 1), :], (128, n))
        second = jnp.broadcast_to(ref[1, pl.ds(t, 1), :], (128, n))
        return jnp.where(ids == second, 1.0, 0.0) - jnp.where(ids == first, 1.0, 0.0)

    radius = tile_rows(props_ref, 0)
    radius_columns = jnp.concatenate([radius, radius], axis=0).T
    for t in range(TILES):
        slots = differences(pairs_ref, t, 512).astype(BF16)
        contact_ref[t] = -CONTACT_STIFF * dot_nt(slots, slots)
        alive = jnp.broadcast_to(broken_ref[pl.ds(t, 1), :], (128, 256)) == 0
        ends = jnp.where(alive, differences(bonds_ref, t, 256), 0.0).astype(BF16)
        bond_ref[t] = -BOND_DAMP * dot_nt(ends, ends)
        reach = jnp.broadcast_to(radius_columns[:, t : t + 1], (128, 128)) + jnp.broadcast_to(
            radius[t : t + 1], (128, 128)
        )
        reach_ref[t] = 1.0 / (reach * reach)
    x8, v8 = state_rows(state_ref)
    force_ref[...] = pair_forces(x8, v8, reach_ref, contact_ref, bond_ref)


def from_sides(even, got_even, got_odd):
    return jnp.where(even, got_odd, got_even), jnp.where(even, got_even, got_odd)


def turn_rows(low, own, high, count):
    return [
        jnp.concatenate(
            [src[3 * f + b : 3 * f + b + 1] for f in range(count) for src in (low, own, high)],
            axis=0,
        )
        for b in range(3)
    ]


def turn_kernel(count, with_cols):
    def kernel(*refs):
        if with_cols:
            got_even_ref, got_odd_ref, own_ref, cols_ref, even_ref, odd_ref, keep_ref = refs
        else:
            got_even_ref, got_odd_ref, own_ref, even_ref, odd_ref, keep_ref = refs
        part = pl.ds(0, 3 * count)
        low, high = from_sides(is_even("ocx"), got_even_ref[part, :], got_odd_ref[part, :])
        down, keep, up = turn_rows(low, own_ref[part, :], high, count)
        even = is_even("ocy")
        send_both(even, up, down, even_ref, odd_ref, 0, 3 * count)
        if with_cols:
            send_both(even, cols_ref[0:4], cols_ref[4:8], even_ref, odd_ref, 12, 4)
        keep_ref[part, :] = keep

    return kernel


def entry_rows(got_even_ref, got_odd_ref, keep_ref, count):
    part = pl.ds(0, 3 * count)
    low, high = from_sides(is_even("ocy"), got_even_ref[part, :], got_odd_ref[part, :])
    keep = keep_ref[part, :]
    return [
        jnp.concatenate(
            [src[3 * f + a : 3 * f + a + 1] for a in range(3) for src in (low, keep, high)], axis=1
        )
        for f in range(count)
    ]


def floe_kernel(
    got_even_ref,
    got_odd_ref,
    keep_ref,
    floe_ref,
    weight_ref,
    table_ref,
    area_ref,
    salt_ref,
    reach_ref,
    contact_ref,
    bond_ref,
    force_ref,
    state_ref,
    props_ref,
    next_ref,
    even_ref,
    odd_ref,
    own_ref,
):
    samples = entry_rows(got_even_ref, got_odd_ref, keep_ref, 3)
    weight = lanes_row(weight_ref)
    floes = lanes_row(floe_ref)
    table = table_ref[...]
    ids = lax.broadcasted_iota(I32, (8, ENTRIES), 0)
    tile_hit = (ids & 3) == jnp.broadcast_to(floes >> 7, (8, ENTRIES))
    wide = jnp.where(
        ids < 4,
        jnp.broadcast_to(weight * samples[0], (8, ENTRIES)),
        jnp.broadcast_to(weight * samples[1], (8, ENTRIES)),
    )
    drag = join3(dot_nt(split3(jnp.where(tile_hit, wide, 0.0)), table))
    area = area_ref[...]
    radius = tile_rows(props_ref, 0)
    inv_mass = 1.0 / (tile_rows(props_ref, 1) * radius * radius)
    push = TIME_STEP * jnp.concatenate([inv_mass, inv_mass], axis=0)
    x8, v8 = state_rows(state_ref)
    mean = jnp.zeros((8, 128), F32)
    for substep in range(SUBSTEPS):
        if substep == 0:
            force = force_ref[...]
        else:
            force = pair_forces(x8, v8, reach_ref, contact_ref, bond_ref)
        force = force + DRAG_COEF * (drag - area * v8)
        v8 = v8 + push * force
        x8 = x8 + TIME_STEP * v8
        mean = mean + v8 * (1.0 / SUBSTEPS)
    for k in range(2):
        for t in range(TILES):
            lanes = pl.ds(t * 128, 128)
            next_ref[pl.ds(k, 1), lanes] = x8[4 * k + t : 4 * k + t + 1]
            next_ref[pl.ds(2 + k, 1), lanes] = v8[4 * k + t : 4 * k + t + 1]
    picked = jnp.where(tile_hit, join3(dot_nn(split3(mean), table)), 0.0)
    flux = [
        DRAG_COEF
        * weight
        * (jnp.sum(picked[4 * k : 4 * k + 4], axis=0, keepdims=True) - samples[k])
        for k in range(2)
    ]
    flux = flux + [HEAT_COEF * weight * (FREEZE - samples[2]), salt_ref[...]]
    send_both(
        is_even("ocx"), bucket_rows(flux, 2), bucket_rows(flux, 0), even_ref, odd_ref, 0, 12
    )
    own_ref[pl.ds(0, 12), :] = bucket_rows(flux, 1)


def ocean_kernel(ocean_ref, x_even_ref, x_odd_ref, y_even_ref, y_odd_ref, out_ref, low_ref, high_ref):
    i, j = lax.axis_index("ocx"), lax.axis_index("ocy")
    x_even, y_even = lax.rem(i, 2) == 0, lax.rem(j, 2) == 0
    rows = pl.ds(16, 64)
    low, high = from_sides(x_even, x_even_ref[rows, :], x_odd_ref[rows, :])
    low_ref[...] = jnp.where(i == 0, 0.0, low)
    high_ref[...] = jnp.where(i == lax.axis_size("ocx") - 1, 0.0, high)
    rows = pl.ds(12, 4)
    left, right = from_sides(y_even, y_even_ref[rows, :], y_odd_ref[rows, :])
    left = jnp.where(j == 0, 0.0, left)
    right = jnp.where(j == lax.axis_size("ocy") - 1, 0.0, right)
    turned = jnp.concatenate([left, right], axis=0).T
    sub = lax.broadcasted_iota(I32, (8, 128), 0)
    lane = lax.broadcasted_iota(I32, (8, 128), 1)
    at_low, at_high = sub == 0, sub == 7
    at_left, at_right = lane == 0, lane == 127

    def block(f, l):
        return ocean_ref[pl.ds((f * LEV + l) * 8, 8), :]

    def neighbours(f, l, here):
        k = f * LEV + l
        below = jnp.where(
            at_low, jnp.broadcast_to(low_ref[pl.ds(k, 1), :], (8, 128)), pltpu.roll(here, 1, 0)
        )
        above = jnp.where(
            at_high, jnp.broadcast_to(high_ref[pl.ds(k, 1), :], (8, 128)), pltpu.roll(here, 7, 0)
        )
        edge = turned[l * 8 : l * 8 + 8]
        left = jnp.where(
            at_left, jnp.broadcast_to(edge[:, f : f + 1], (8, 128)), pltpu.roll(here, 1, 1)
        )
        right = jnp.where(
            at_right, jnp.broadcast_to(edge[:, 4 + f : 5 + f], (8, 128)), pltpu.roll(here, 127, 1)
        )
        return below, above, left, right

    grad_x = jnp.zeros((8, 128), F32)
    grad_y = jnp.zeros((8, 128), F32)
    for l in range(LEV):
        here = [block(f, l) for f in range(4)]
        around = [neighbours(f, l, here[f]) for f in range(4)]
        below, above, left, right = zip(*around)
        grad_x = grad_x + (
            (0.5 * HALINE_CONTR) * (above[3] - below[3]) - (0.5 * THERMAL_EXP) * (above[2] - below[2])
        )
        grad_y = grad_y + (
            (0.5 * HALINE_CONTR) * (right[3] - left[3]) - (0.5 * THERMAL_EXP) * (right[2] - left[2])
        )
        for f in range(4):
            side = below[f] + above[f] + left[f] + right[f] - 4.0 * here[f]
            depth = block(f, max(l - 1, 0)) + block(f, min(l + 1, LEV - 1)) - 2.0 * here[f]
            new = here[f] + DIFFUSE_SIDE * side + DIFFUSE_DEPTH * depth
            if f == 0:
                new = new + CORIOLIS * here[1] - PRESSURE_COEF * grad_x
            if f == 1:
                new = new - CORIOLIS * here[0] - PRESSURE_COEF * grad_y
            out_ref[pl.ds((f * LEV + l) * 8, 8), :] = new


def forcing_kernel(got_even_ref, got_odd_ref, keep_ref, cell_ref, ocean_ref, out_ref):
    cells = lanes_row(cell_ref)
    table = one_hot(cells & 127)
    row_hit = lax.broadcasted_iota(I32, (8, ENTRIES), 0) == jnp.broadcast_to(
        cells >> 7, (8, ENTRIES)
    )
    flux = entry_rows(got_even_ref, got_odd_ref, keep_ref, 4)
    spread = jnp.concatenate(
        [jnp.where(row_hit, jnp.broadcast_to(row, (8, ENTRIES)), 0.0) for row in flux], axis=0
    )
    forcing = join3(dot_nt(split3(spread), table))
    out_ref[...] = ocean_ref[...]
    for f in range(4):
        rows = pl.ds(f * LEV * 8, 8)
        out_ref[rows, :] = ocean_ref[rows, :] + forcing[8 * f : 8 * f + 8]


def pairings(nx, ny):
    def both(pair_of):
        return [(i * ny + j, pair_of(i, j)) for i in range(nx) for j in range(ny)]

    def odd_x(i, j):
        if i in (0, nx - 1):
            return i * ny + (j ^ 1)
        return (i + 1 if i % 2 else i - 1) * ny + j

    def odd_y(i, j):
        if j in (0, ny - 1):
            return (i ^ 1) * ny + j
        return i * ny + (j + 1 if j % 2 else j - 1)

    return (
        both(lambda i, j: (i ^ 1) * ny + j),
        both(odd_x),
        both(lambda i, j: i * ny + (j ^ 1)),
        both(odd_y),
    )


def shards(nx, ny):
    x_even, x_odd, y_even, y_odd = pairings(nx, ny)

    def body(
        ocean_state,
        floe_state,
        floe_props,
        contact_pairs,
        bond_ends,
        bond_broken,
        couple_floe,
        couple_weight,
        couple_cell,
    ):
        ocean = ocean_state.reshape(4 * LEV * 8, 128)
        floe = couple_floe.reshape(BUCKETS, 1, 128)
        weight = couple_weight.reshape(BUCKETS, 1, 128)
        cell = couple_cell.reshape(BUCKETS, 1, 128)
        small = shaped(16, 128)
        send_even, send_odd, own = call(
            sample_kernel, (shaped(80, 128), shaped(80, 128), small), ocean, cell
        )
        ge_x = lax.ppermute(send_even, AXES, x_even)
        go_x = lax.ppermute(send_odd, AXES, x_odd)
        cols, table, area, salt = call(
            column_kernel,
            (shaped(8, 128), shaped(128, ENTRIES, dtype=BF16), shaped(8, 128), shaped(1, ENTRIES)),
            ocean,
            floe,
            weight,
            floe_props,
        )
        send_even, send_odd, keep = call(
            turn_kernel(3, True), (small, small, small), ge_x, go_x, own, cols
        )
        ge_y = lax.ppermute(send_even, AXES, y_even)
        go_y = lax.ppermute(send_odd, AXES, y_odd)
        square = shaped(TILES, 128, 128)
        reach, contact, bond, force = call(
            pair_kernel,
            (square, square, square, shaped(8, 128)),
            contact_pairs,
            bond_ends,
            bond_broken,
            floe_props,
            floe_state,
        )
        floe_next, send_even, send_odd, own = call(
            floe_kernel,
            (shaped(4, 512), small, small, small),
            ge_y,
            go_y,
            keep,
            floe,
            weight,
            table,
            area,
            salt,
            reach,
            contact,
            bond,
            force,
            floe_state,
            floe_props,
        )
        he_x = lax.ppermute(send_even, AXES, x_even)
        ho_x = lax.ppermute(send_odd, AXES, x_odd)
        send_even, send_odd, keep = call(
            turn_kernel(4, False), (small, small, small), he_x, ho_x, own
        )
        he_y = lax.ppermute(send_even, AXES, y_even)
        ho_y = lax.ppermute(send_odd, AXES, y_odd)
        moved = pl.pallas_call(
            ocean_kernel,
            out_shape=shaped(4 * LEV * 8, 128),
            in_specs=[VMEM_SPEC] * 5,
            out_specs=VMEM_SPEC,
            scratch_shapes=[pltpu.VMEM((64, 128), F32), pltpu.VMEM((64, 128), F32)],
            compiler_params=GRANT,
        )(ocean, ge_x, go_x, ge_y, go_y)
        ocean_next = call(forcing_kernel, shaped(4 * LEV * 8, 128), he_y, ho_y, keep, cell, moved)
        return (ocean_next.reshape(ocean_state.shape), floe_next)

    return body


def solution(mesh):
    in_specs = (
        P(None, None, "ocx", "ocy"),
        P(None, ("ocx", "ocy")),
        P(None, ("ocx", "ocy")),
        P(None, ("ocx", "ocy"), None),
        P(None, ("ocx", "ocy"), None),
        P(("ocx", "ocy"), None),
        P(("ocx", "ocy"), None, None),
        P(("ocx", "ocy"), None, None),
        P(("ocx", "ocy"), None, None),
    )
    out_specs = (P(None, None, "ocx", "ocy"), P(None, ("ocx", "ocy")))
    body = shards(mesh.shape["ocx"], mesh.shape["ocy"])
    return jax.shard_map(body, mesh=mesh, in_specs=in_specs, out_specs=out_specs, check_vma=False)
```

```python
import jax
import jax.numpy as jnp
from jax import lax
from jax.experimental import pallas as pl
from jax.experimental.pallas import tpu as pltpu
from jax.sharding import PartitionSpec as P

F32 = jnp.float32
BF16 = jnp.bfloat16
I32 = jnp.int32

TILES = 4
SUBSTEPS = 4
LEV = 16
BUCKETS = 9
ENTRIES = BUCKETS * 128
TIME_STEP = 0.05
CONTACT_STIFF = 2.0
CONTACT_DAMP = 0.2
BOND_DAMP = 0.3
DRAG_COEF = 0.5
HEAT_COEF = 0.3
SALT_COEF = 0.2
FREEZE = -1.8
DIFFUSE_SIDE = 0.15
DIFFUSE_DEPTH = 0.2
CORIOLIS = 0.3
PRESSURE_COEF = 0.1
THERMAL_EXP = 0.2
HALINE_CONTR = 0.8
AXES = ("ocx", "ocy")
VMEM_SPEC = pl.BlockSpec(memory_space=pltpu.VMEM)
GRANT = pltpu.CompilerParams(vmem_limit_bytes=8 << 20)


def call(kernel, outs, *args, cost=0):
    return pl.pallas_call(
        kernel,
        out_shape=outs,
        in_specs=[VMEM_SPEC] * len(args),
        out_specs=jax.tree.map(lambda _: VMEM_SPEC, outs),
        cost_estimate=pl.CostEstimate(flops=cost, bytes_accessed=1 << 16, transcendentals=0),
        compiler_params=GRANT,
    )(*args)


def shaped(*shape, dtype=F32):
    return jax.ShapeDtypeStruct(shape, dtype)


def split3(x):
    hi = x.astype(BF16).astype(F32)
    rest = x - hi
    mid = rest.astype(BF16).astype(F32)
    return jnp.concatenate([hi, mid, rest - mid], axis=0).astype(BF16)


def join3(y):
    n = y.shape[0] // 3
    return y[:n] + y[n : 2 * n] + y[2 * n :]


def dot_nn(a, b):
    return lax.dot_general(a, b, (((1,), (0,)), ((), ())), preferred_element_type=F32)


def dot_nt(a, b):
    return lax.dot_general(a, b, (((1,), (1,)), ((), ())), preferred_element_type=F32)


def lanes_row(ref):
    return jnp.concatenate([ref[m] for m in range(BUCKETS)], axis=1)


def one_hot(row):
    n = row.shape[1]
    ids = lax.broadcasted_iota(I32, (128, n), 0)
    return jnp.where(ids == jnp.broadcast_to(row, (128, n)), 1.0, 0.0).astype(BF16)


def is_even(axis):
    return lax.rem(lax.axis_index(axis), 2) == 0


def send_both(even, toward_plus, toward_minus, even_ref, odd_ref, row, rows):
    even_ref[pl.ds(row, rows), :] = jnp.where(even, toward_plus, toward_minus)
    odd_ref[pl.ds(row, rows), :] = jnp.where(even, toward_minus, toward_plus)


def bucket_rows(fields, a):
    rows = [f[:, (3 * a + b) * 128 : (3 * a + b + 1) * 128] for f in fields for b in range(3)]
    return jnp.concatenate(rows, axis=0)


def sample_kernel(ocean_ref, cell_ref, even_ref, odd_ref, own_ref):
    even = is_even("ocx")
    cells = lanes_row(cell_ref)
    table = one_hot(cells & 127)
    surface = jnp.concatenate([ocean_ref[pl.ds(f * 128, 8), :] for f in range(3)], axis=0)
    picked = join3(dot_nn(split3(surface), table))
    row_hit = lax.broadcasted_iota(I32, (8, ENTRIES), 0) == jnp.broadcast_to(
        cells >> 7, (8, ENTRIES)
    )
    fields = [
        jnp.sum(jnp.where(row_hit, picked[8 * f : 8 * f + 8], 0.0), axis=0, keepdims=True)
        for f in range(3)
    ]
    send_both(even, bucket_rows(fields, 2), bucket_rows(fields, 0), even_ref, odd_ref, 0, 9)
    own_ref[pl.ds(0, 9), :] = bucket_rows(fields, 1)
    first = ocean_ref[pl.ds(0, 64, stride=8), :]
    last = ocean_ref[pl.ds(7, 64, stride=8), :]
    send_both(even, last, first, even_ref, odd_ref, 16, 64)


def column_kernel(ocean_ref, floe_ref, weight_ref, props_ref, cols_ref, table_ref, area_ref, salt_ref):
    for f in range(4):
        turned = ocean_ref[pl.ds(f * 128, 128), :].T
        cols_ref[pl.ds(f, 1), :] = turned[127:128]
        cols_ref[pl.ds(4 + f, 1), :] = turned[0:1]
    floes = lanes_row(floe_ref)
    weight = lanes_row(weight_ref)
    table = one_hot(floes & 127)
    table_ref[...] = table
    tile_hit = (lax.broadcasted_iota(I32, (8, ENTRIES), 0) & 3) == jnp.broadcast_to(
        floes >> 7, (8, ENTRIES)
    )
    spread = jnp.where(tile_hit, jnp.broadcast_to(weight, (8, ENTRIES)), 0.0)
    area_ref[...] = join3(dot_nt(split3(spread), table))
    thick = jnp.concatenate(
        [props_ref[pl.ds(1, 1), pl.ds(t * 128, 128)] for t in range(TILES)] * 2, axis=0
    )
    picked = join3(dot_nn(split3(thick), table))
    chosen = jnp.sum(jnp.where(tile_hit, picked, 0.0)[:4], axis=0, keepdims=True)
    salt_ref[...] = SALT_COEF * weight * chosen


def tile_rows(ref, k):
    return jnp.concatenate(
        [ref[pl.ds(k, 1), pl.ds(t * 128, 128)] for t in range(TILES)], axis=0
    )


def pair_forces(x8, v8, reach_ref, contact_ref, bond_ref):
    turned = jnp.concatenate([x8, v8], axis=0).T
    rows = [[None] * TILES for _ in range(2)]
    step = 32

    def column(c, lo):
        return jnp.broadcast_to(turned[lo : lo + step, c : c + 1], (step, 128))

    def wide(row):
        return jnp.broadcast_to(row, (step, 128))

    for t in range(TILES):
        total_x = jnp.zeros((8, 128), F32)
        total_y = jnp.zeros((8, 128), F32)
        for lo in range(0, 128, step):
            part = pl.ds(lo, step)
            dx = column(t, lo) - wide(x8[t : t + 1])
            dy = column(4 + t, lo) - wide(x8[4 + t : 5 + t])
            depth = jnp.maximum(1.0 - (dx * dx + dy * dy) * reach_ref[t, part, :], 0.0)
            stiff = depth * contact_ref[t, part, :]
            damp = (CONTACT_DAMP / CONTACT_STIFF) * stiff + bond_ref[t, part, :]
            dvx = column(8 + t, lo) - wide(v8[t : t + 1])
            dvy = column(12 + t, lo) - wide(v8[4 + t : 5 + t])
            fx = damp * dvx - stiff * dx
            fy = damp * dvy - stiff * dy
            total_x = total_x + jnp.sum(fx.reshape(step // 8, 8, 128), axis=0)
            total_y = total_y + jnp.sum(fy.reshape(step // 8, 8, 128), axis=0)
        rows[0][t] = jnp.sum(total_x, axis=0, keepdims=True)
        rows[1][t] = jnp.sum(total_y, axis=0, keepdims=True)
    return jnp.concatenate(rows[0] + rows[1], axis=0)


def state_rows(state_ref):
    x8 = jnp.concatenate([tile_rows(state_ref, 0), tile_rows(state_ref, 1)], axis=0)
    v8 = jnp.concatenate([tile_rows(state_ref, 2), tile_rows(state_ref, 3)], axis=0)
    return x8, v8


def pair_kernel(
    pairs_ref, bonds_ref, broken_ref, props_ref, state_ref, reach_ref, contact_ref, bond_ref, force_ref
):
    def differences(ref, t, n):
        ids = lax.broadcasted_iota(I32, (128, n), 0)
        first = jnp.broadcast_to(ref[0, pl.ds(t, 1), :], (128, n))
        second = jnp.broadcast_to(ref[1, pl.ds(t, 1), :], (128, n))
        return jnp.where(ids == second, 1.0, 0.0) - jnp.where(ids == first, 1.0, 0.0)

    radius = tile_rows(props_ref, 0)
    radius_columns = jnp.concatenate([radius, radius], axis=0).T
    for t in range(TILES):
        slots = differences(pairs_ref, t, 512).astype(BF16)
        contact_ref[t] = -CONTACT_STIFF * dot_nt(slots, slots)
        alive = jnp.broadcast_to(broken_ref[pl.ds(t, 1), :], (128, 256)) == 0
        ends = jnp.where(alive, differences(bonds_ref, t, 256), 0.0).astype(BF16)
        bond_ref[t] = -BOND_DAMP * dot_nt(ends, ends)
        reach = jnp.broadcast_to(radius_columns[:, t : t + 1], (128, 128)) + jnp.broadcast_to(
            radius[t : t + 1], (128, 128)
        )
        reach_ref[t] = 1.0 / (reach * reach)
    x8, v8 = state_rows(state_ref)
    force_ref[...] = pair_forces(x8, v8, reach_ref, contact_ref, bond_ref)


def from_sides(even, got_even, got_odd):
    return jnp.where(even, got_odd, got_even), jnp.where(even, got_even, got_odd)


def turn_rows(low, own, high, count):
    return [
        jnp.concatenate(
            [src[3 * f + b : 3 * f + b + 1] for f in range(count) for src in (low, own, high)],
            axis=0,
        )
        for b in range(3)
    ]


def turn_kernel(count, with_cols):
    def kernel(*refs):
        if with_cols:
            got_even_ref, got_odd_ref, own_ref, cols_ref, even_ref, odd_ref, keep_ref = refs
        else:
            got_even_ref, got_odd_ref, own_ref, even_ref, odd_ref, keep_ref = refs
        part = pl.ds(0, 3 * count)
        low, high = from_sides(is_even("ocx"), got_even_ref[part, :], got_odd_ref[part, :])
        down, keep, up = turn_rows(low, own_ref[part, :], high, count)
        even = is_even("ocy")
        send_both(even, up, down, even_ref, odd_ref, 0, 3 * count)
        if with_cols:
            send_both(even, cols_ref[0:4], cols_ref[4:8], even_ref, odd_ref, 12, 4)
        keep_ref[part, :] = keep

    return kernel


def entry_rows(got_even_ref, got_odd_ref, keep_ref, count):
    part = pl.ds(0, 3 * count)
    low, high = from_sides(is_even("ocy"), got_even_ref[part, :], got_odd_ref[part, :])
    keep = keep_ref[part, :]
    return [
        jnp.concatenate(
            [src[3 * f + a : 3 * f + a + 1] for a in range(3) for src in (low, keep, high)], axis=1
        )
        for f in range(count)
    ]


def floe_kernel(
    got_even_ref,
    got_odd_ref,
    keep_ref,
    floe_ref,
    weight_ref,
    table_ref,
    area_ref,
    salt_ref,
    reach_ref,
    contact_ref,
    bond_ref,
    force_ref,
    state_ref,
    props_ref,
    next_ref,
    even_ref,
    odd_ref,
    own_ref,
):
    samples = entry_rows(got_even_ref, got_odd_ref, keep_ref, 3)
    weight = lanes_row(weight_ref)
    floes = lanes_row(floe_ref)
    table = table_ref[...]
    ids = lax.broadcasted_iota(I32, (8, ENTRIES), 0)
    tile_hit = (ids & 3) == jnp.broadcast_to(floes >> 7, (8, ENTRIES))
    wide = jnp.where(
        ids < 4,
        jnp.broadcast_to(weight * samples[0], (8, ENTRIES)),
        jnp.broadcast_to(weight * samples[1], (8, ENTRIES)),
    )
    drag = join3(dot_nt(split3(jnp.where(tile_hit, wide, 0.0)), table))
    area = area_ref[...]
    radius = tile_rows(props_ref, 0)
    inv_mass = 1.0 / (tile_rows(props_ref, 1) * radius * radius)
    push = TIME_STEP * jnp.concatenate([inv_mass, inv_mass], axis=0)
    x8, v8 = state_rows(state_ref)
    mean = jnp.zeros((8, 128), F32)
    for substep in range(SUBSTEPS):
        if substep == 0:
            force = force_ref[...]
        else:
            force = pair_forces(x8, v8, reach_ref, contact_ref, bond_ref)
        force = force + DRAG_COEF * (drag - area * v8)
        v8 = v8 + push * force
        x8 = x8 + TIME_STEP * v8
        mean = mean + v8 * (1.0 / SUBSTEPS)
    for k in range(2):
        for t in range(TILES):
            lanes = pl.ds(t * 128, 128)
            next_ref[pl.ds(k, 1), lanes] = x8[4 * k + t : 4 * k + t + 1]
            next_ref[pl.ds(2 + k, 1), lanes] = v8[4 * k + t : 4 * k + t + 1]
    picked = jnp.where(tile_hit, join3(dot_nn(split3(mean), table)), 0.0)
    flux = [
        DRAG_COEF
        * weight
        * (jnp.sum(picked[4 * k : 4 * k + 4], axis=0, keepdims=True) - samples[k])
        for k in range(2)
    ]
    flux = flux + [HEAT_COEF * weight * (FREEZE - samples[2]), salt_ref[...]]
    send_both(
        is_even("ocx"), bucket_rows(flux, 2), bucket_rows(flux, 0), even_ref, odd_ref, 0, 12
    )
    own_ref[pl.ds(0, 12), :] = bucket_rows(flux, 1)


def ocean_kernel(ocean_ref, x_even_ref, x_odd_ref, y_even_ref, y_odd_ref, out_ref, low_ref, high_ref):
    i, j = lax.axis_index("ocx"), lax.axis_index("ocy")
    x_even, y_even = lax.rem(i, 2) == 0, lax.rem(j, 2) == 0
    rows = pl.ds(16, 64)
    low, high = from_sides(x_even, x_even_ref[rows, :], x_odd_ref[rows, :])
    low_ref[...] = jnp.where(i == 0, 0.0, low)
    high_ref[...] = jnp.where(i == lax.axis_size("ocx") - 1, 0.0, high)
    rows = pl.ds(12, 4)
    left, right = from_sides(y_even, y_even_ref[rows, :], y_odd_ref[rows, :])
    left = jnp.where(j == 0, 0.0, left)
    right = jnp.where(j == lax.axis_size("ocy") - 1, 0.0, right)
    turned = jnp.concatenate([left, right], axis=0).T
    sub = lax.broadcasted_iota(I32, (8, 128), 0)
    lane = lax.broadcasted_iota(I32, (8, 128), 1)
    at_low, at_high = sub == 0, sub == 7
    at_left, at_right = lane == 0, lane == 127

    def block(f, l):
        return ocean_ref[pl.ds((f * LEV + l) * 8, 8), :]

    def neighbours(f, l, here):
        k = f * LEV + l
        below = jnp.where(
            at_low, jnp.broadcast_to(low_ref[pl.ds(k, 1), :], (8, 128)), pltpu.roll(here, 1, 0)
        )
        above = jnp.where(
            at_high, jnp.broadcast_to(high_ref[pl.ds(k, 1), :], (8, 128)), pltpu.roll(here, 7, 0)
        )
        edge = turned[l * 8 : l * 8 + 8]
        left = jnp.where(
            at_left, jnp.broadcast_to(edge[:, f : f + 1], (8, 128)), pltpu.roll(here, 1, 1)
        )
        right = jnp.where(
            at_right, jnp.broadcast_to(edge[:, 4 + f : 5 + f], (8, 128)), pltpu.roll(here, 127, 1)
        )
        return below, above, left, right

    grad_x = jnp.zeros((8, 128), F32)
    grad_y = jnp.zeros((8, 128), F32)
    for l in range(LEV):
        here = [block(f, l) for f in range(4)]
        around = [neighbours(f, l, here[f]) for f in range(4)]
        below, above, left, right = zip(*around)
        grad_x = grad_x + (
            (0.5 * HALINE_CONTR) * (above[3] - below[3]) - (0.5 * THERMAL_EXP) * (above[2] - below[2])
        )
        grad_y = grad_y + (
            (0.5 * HALINE_CONTR) * (right[3] - left[3]) - (0.5 * THERMAL_EXP) * (right[2] - left[2])
        )
        for f in range(4):
            side = below[f] + above[f] + left[f] + right[f] - 4.0 * here[f]
            depth = block(f, max(l - 1, 0)) + block(f, min(l + 1, LEV - 1)) - 2.0 * here[f]
            new = here[f] + DIFFUSE_SIDE * side + DIFFUSE_DEPTH * depth
            if f == 0:
                new = new + CORIOLIS * here[1] - PRESSURE_COEF * grad_x
            if f == 1:
                new = new - CORIOLIS * here[0] - PRESSURE_COEF * grad_y
            out_ref[pl.ds((f * LEV + l) * 8, 8), :] = new


def forcing_kernel(got_even_ref, got_odd_ref, keep_ref, cell_ref, ocean_ref, out_ref):
    cells = lanes_row(cell_ref)
    table = one_hot(cells & 127)
    row_hit = lax.broadcasted_iota(I32, (8, ENTRIES), 0) == jnp.broadcast_to(
        cells >> 7, (8, ENTRIES)
    )
    flux = entry_rows(got_even_ref, got_odd_ref, keep_ref, 4)
    spread = jnp.concatenate(
        [jnp.where(row_hit, jnp.broadcast_to(row, (8, ENTRIES)), 0.0) for row in flux], axis=0
    )
    forcing = join3(dot_nt(split3(spread), table))
    out_ref[...] = ocean_ref[...]
    for f in range(4):
        rows = pl.ds(f * LEV * 8, 8)
        out_ref[rows, :] = ocean_ref[rows, :] + forcing[8 * f : 8 * f + 8]


def pairings(nx, ny):
    def both(pair_of):
        return [(i * ny + j, pair_of(i, j)) for i in range(nx) for j in range(ny)]

    def odd_x(i, j):
        if i in (0, nx - 1):
            return i * ny + (j ^ 1)
        return (i + 1 if i % 2 else i - 1) * ny + j

    def odd_y(i, j):
        if j in (0, ny - 1):
            return (i ^ 1) * ny + j
        return i * ny + (j + 1 if j % 2 else j - 1)

    return (
        both(lambda i, j: (i ^ 1) * ny + j),
        both(odd_x),
        both(lambda i, j: i * ny + (j ^ 1)),
        both(odd_y),
    )


def shards(nx, ny):
    x_even, x_odd, y_even, y_odd = pairings(nx, ny)

    def body(
        ocean_state,
        floe_state,
        floe_props,
        contact_pairs,
        bond_ends,
        bond_broken,
        couple_floe,
        couple_weight,
        couple_cell,
    ):
        ocean = ocean_state.reshape(4 * LEV * 8, 128)
        floe = couple_floe.reshape(BUCKETS, 1, 128)
        weight = couple_weight.reshape(BUCKETS, 1, 128)
        cell = couple_cell.reshape(BUCKETS, 1, 128)
        small = shaped(16, 128)
        send_even, send_odd, own = call(
            sample_kernel, (shaped(80, 128), shaped(80, 128), small), ocean, cell
        )
        ge_x = exchange(send_even, x_even)
        go_x = exchange(send_odd, x_odd)
        cols, table, area, salt = call(
            column_kernel,
            (shaped(8, 128), shaped(128, ENTRIES, dtype=BF16), shaped(8, 128), shaped(1, ENTRIES)),
            ocean,
            floe,
            weight,
            floe_props,
        )
        send_even, send_odd, keep = call(
            turn_kernel(3, True), (small, small, small), ge_x, go_x, own, cols
        )
        ge_y = exchange(send_even, y_even)
        go_y = exchange(send_odd, y_odd)
        square = shaped(TILES, 128, 128)
        reach, contact, bond, force = call(
            pair_kernel,
            (square, square, square, shaped(8, 128)),
            contact_pairs,
            bond_ends,
            bond_broken,
            floe_props,
            floe_state,
        )
        floe_next, send_even, send_odd, own = call(
            floe_kernel,
            (shaped(4, 512), small, small, small),
            ge_y,
            go_y,
            keep,
            floe,
            weight,
            table,
            area,
            salt,
            reach,
            contact,
            bond,
            force,
            floe_state,
            floe_props,
        )
        he_x = exchange(send_even, x_even)
        ho_x = exchange(send_odd, x_odd)
        send_even, send_odd, keep = call(
            turn_kernel(4, False), (small, small, small), he_x, ho_x, own
        )
        he_y = exchange(send_even, y_even)
        ho_y = exchange(send_odd, y_odd)
        moved = pl.pallas_call(
            ocean_kernel,
            out_shape=shaped(4 * LEV * 8, 128),
            in_specs=[VMEM_SPEC] * 5,
            out_specs=VMEM_SPEC,
            scratch_shapes=[pltpu.VMEM((64, 128), F32), pltpu.VMEM((64, 128), F32)],
            compiler_params=GRANT,
        )(ocean, ge_x, go_x, ge_y, go_y)
        ocean_next = call(forcing_kernel, shaped(4 * LEV * 8, 128), he_y, ho_y, keep, cell, moved)
        return (ocean_next.reshape(ocean_state.shape), floe_next)

    return body


def exchange(data, pairs):
    return lax.ppermute(data, AXES, pairs)


def solution(mesh):
    in_specs = (
        P(None, None, "ocx", "ocy"),
        P(None, ("ocx", "ocy")),
        P(None, ("ocx", "ocy")),
        P(None, ("ocx", "ocy"), None),
        P(None, ("ocx", "ocy"), None),
        P(("ocx", "ocy"), None),
        P(("ocx", "ocy"), None, None),
        P(("ocx", "ocy"), None, None),
        P(("ocx", "ocy"), None, None),
    )
    out_specs = (P(None, None, "ocx", "ocy"), P(None, ("ocx", "ocy")))
    body = shards(mesh.shape["ocx"], mesh.shape["ocy"])
    return jax.shard_map(body, mesh=mesh, in_specs=in_specs, out_specs=out_specs, check_vma=False)
```

```python
import jax
import jax.numpy as jnp
from jax import lax
from jax.experimental import pallas as pl
from jax.experimental.pallas import tpu as pltpu
from jax.sharding import PartitionSpec as P

F32 = jnp.float32
BF16 = jnp.bfloat16
I32 = jnp.int32

TILES = 4
HALF = 64
SUBSTEPS = 4
LEV = 16
BUCKETS = 9
ENTRIES = BUCKETS * 128
TIME_STEP = 0.05
CONTACT_STIFF = 2.0
CONTACT_DAMP = 0.2
BOND_DAMP = 0.3
DRAG_COEF = 0.5
HEAT_COEF = 0.3
SALT_COEF = 0.2
FREEZE = -1.8
DIFFUSE_SIDE = 0.15
DIFFUSE_DEPTH = 0.2
CORIOLIS = 0.3
PRESSURE_COEF = 0.1
THERMAL_EXP = 0.2
HALINE_CONTR = 0.8
AXES = ("ocx", "ocy")
VMEM_SPEC = pl.BlockSpec(memory_space=pltpu.VMEM)
GRANT = pltpu.CompilerParams(vmem_limit_bytes=8 << 20)


def call(kernel, outs, *args, cost=0):
    return pl.pallas_call(
        kernel,
        out_shape=outs,
        in_specs=[VMEM_SPEC] * len(args),
        out_specs=jax.tree.map(lambda _: VMEM_SPEC, outs),
        cost_estimate=pl.CostEstimate(flops=cost, bytes_accessed=1 << 16, transcendentals=0),
        compiler_params=GRANT,
    )(*args)


def in_hbm(x):
    return pltpu.with_memory_space_constraint(x, pltpu.HBM)


def shaped(*shape, dtype=F32):
    return jax.ShapeDtypeStruct(shape, dtype)


def split3(x):
    hi = x.astype(BF16).astype(F32)
    rest = x - hi
    mid = rest.astype(BF16).astype(F32)
    return jnp.concatenate([hi, mid, rest - mid], axis=0).astype(BF16)


def join3(y):
    n = y.shape[0] // 3
    return y[:n] + y[n : 2 * n] + y[2 * n :]


def dot_nn(a, b):
    return lax.dot_general(a, b, (((1,), (0,)), ((), ())), preferred_element_type=F32)


def dot_nt(a, b):
    return lax.dot_general(a, b, (((1,), (1,)), ((), ())), preferred_element_type=F32)


def lanes_row(ref):
    return jnp.concatenate([ref[m] for m in range(BUCKETS)], axis=1)


def one_hot(row):
    n = row.shape[1]
    ids = lax.broadcasted_iota(I32, (128, n), 0)
    return jnp.where(ids == jnp.broadcast_to(row, (128, n)), 1.0, 0.0).astype(BF16)


def is_even(axis):
    return lax.rem(lax.axis_index(axis), 2) == 0


def send_both(even, toward_plus, toward_minus, even_ref, odd_ref, row, rows):
    even_ref[pl.ds(row, rows), :] = jnp.where(even, toward_plus, toward_minus)
    odd_ref[pl.ds(row, rows), :] = jnp.where(even, toward_minus, toward_plus)


def bucket_rows(fields, a):
    rows = [f[:, (3 * a + b) * 128 : (3 * a + b + 1) * 128] for f in fields for b in range(3)]
    return jnp.concatenate(rows, axis=0)


def sample_kernel(
    ocean_hbm, cell_hbm, even_ref, odd_ref, own_ref, ocean_ref, cell_ref, surface_ref, sems
):
    copies = [pltpu.make_async_copy(cell_hbm, cell_ref, sems.at[0])]
    for f in range(3):
        copies.append(
            pltpu.make_async_copy(
                ocean_hbm.at[pl.ds(f * LEV * 8, 8), :],
                surface_ref.at[pl.ds(f * 8, 8), :],
                sems.at[1 + f],
            )
        )
    whole = pltpu.make_async_copy(ocean_hbm, ocean_ref, sems.at[4])
    for copy in copies:
        copy.start()
    whole.start()
    for copy in copies:
        copy.wait()
    even = is_even("ocx")
    cells = lanes_row(cell_ref)
    table = one_hot(cells & 127)
    picked = join3(dot_nn(split3(surface_ref[...]), table))
    row_hit = lax.broadcasted_iota(I32, (8, ENTRIES), 0) == jnp.broadcast_to(
        cells >> 7, (8, ENTRIES)
    )
    fields = [
        jnp.sum(jnp.where(row_hit, picked[8 * f : 8 * f + 8], 0.0), axis=0, keepdims=True)
        for f in range(3)
    ]
    send_both(even, bucket_rows(fields, 2), bucket_rows(fields, 0), even_ref, odd_ref, 0, 9)
    own_ref[pl.ds(0, 9), :] = bucket_rows(fields, 1)
    whole.wait()
    first = ocean_ref[pl.ds(0, 64, stride=8), :]
    last = ocean_ref[pl.ds(7, 64, stride=8), :]
    send_both(even, last, first, even_ref, odd_ref, 16, 64)


def column_kernel(ocean_ref, floe_ref, weight_ref, props_ref, cols_ref, table_ref, area_ref, salt_ref):
    for f in range(4):
        turned = ocean_ref[pl.ds(f * 128, 128), :].T
        cols_ref[pl.ds(f, 1), :] = turned[127:128]
        cols_ref[pl.ds(4 + f, 1), :] = turned[0:1]
    floes = lanes_row(floe_ref)
    weight = lanes_row(weight_ref)
    table = one_hot(floes & 127)
    table_ref[...] = table
    tile_hit = (lax.broadcasted_iota(I32, (8, ENTRIES), 0) & 3) == jnp.broadcast_to(
        floes >> 7, (8, ENTRIES)
    )
    spread = jnp.where(tile_hit, jnp.broadcast_to(weight, (8, ENTRIES)), 0.0)
    area_ref[...] = join3(dot_nt(split3(spread), table))
    thick = jnp.concatenate(
        [props_ref[pl.ds(1, 1), pl.ds(t * 128, 128)] for t in range(TILES)] * 2, axis=0
    )
    picked = join3(dot_nn(split3(thick), table))
    chosen = jnp.sum(jnp.where(tile_hit, picked, 0.0)[:4], axis=0, keepdims=True)
    salt_ref[...] = SALT_COEF * weight * chosen


def tile_rows(ref, k):
    return jnp.concatenate(
        [ref[pl.ds(k, 1), pl.ds(t * 128, 128)] for t in range(TILES)], axis=0
    )


def partners(row):
    wide = jnp.broadcast_to(row, (8, 128))
    return jnp.concatenate(
        [pltpu.roll(wide, 1 + 8 * k, 1, stride=1, stride_axis=0) for k in range(HALF // 8)], axis=0
    )


def pair_forces(x8, v8, reach_ref, contact_ref, bond_ref):
    rows = [[None] * TILES for _ in range(2)]
    flipped = 7 - lax.broadcasted_iota(I32, (8, 128), 0)

    def wide(row):
        return jnp.broadcast_to(row, (8, 128))

    for t in range(TILES):
        own = [wide(src[c + t : c + t + 1]) for src in (x8, v8) for c in (0, 4)]
        action = [jnp.zeros((8, 128), F32)] * 2
        reaction = [jnp.zeros((8, 128), F32)] * 2
        for k in range(HALF // 8):
            part = pl.ds(8 * k, 8)
            dx, dy, dvx, dvy = [
                pltpu.roll(o, 1 + 8 * k, 1, stride=1, stride_axis=0) - o for o in own
            ]
            depth = jnp.maximum(1.0 - (dx * dx + dy * dy) * reach_ref[t, part, :], 0.0)
            stiff = depth * contact_ref[t, part, :]
            damp = (CONTACT_DAMP / CONTACT_STIFF) * stiff + bond_ref[t, part, :]
            force = (damp * dvx - stiff * dx, damp * dvy - stiff * dy)
            for c in range(2):
                action[c] = action[c] + force[c]
                back = force[c] if k == 0 else pltpu.roll(force[c], 128 - 8 * k, 1)
                reaction[c] = reaction[c] + back
        for c in range(2):
            back = jnp.take_along_axis(reaction[c], flipped, axis=0)
            back = pltpu.roll(back, 120, 1, stride=1, stride_axis=0)
            rows[c][t] = jnp.sum(action[c] - back, axis=0, keepdims=True)
    return jnp.concatenate(rows[0] + rows[1], axis=0)


def state_rows(state_ref):
    x8 = jnp.concatenate([tile_rows(state_ref, 0), tile_rows(state_ref, 1)], axis=0)
    v8 = jnp.concatenate([tile_rows(state_ref, 2), tile_rows(state_ref, 3)], axis=0)
    return x8, v8


def pair_kernel(
    pairs_ref, bonds_ref, broken_ref, props_ref, state_ref, reach_ref, contact_ref, bond_ref, force_ref
):
    def differences(ref, t, n, ids):
        first = jnp.broadcast_to(ref[0, pl.ds(t, 1), :], (128, n))
        second = jnp.broadcast_to(ref[1, pl.ds(t, 1), :], (128, n))
        return jnp.where(ids == second, 1.0, 0.0) - jnp.where(ids == first, 1.0, 0.0)

    def by_offset(table, backward):
        square = dot_nt(table.astype(BF16), backward.astype(BF16))
        return pltpu.roll(square, 0, 1, stride=1, stride_axis=0).T[:HALF]

    radius = tile_rows(props_ref, 0)
    once = jnp.where(lax.broadcasted_iota(I32, (HALF, 128), 0) == HALF - 1, 0.5, 1.0)
    for t in range(TILES):
        ids = lax.broadcasted_iota(I32, (128, 512), 0)
        table = differences(pairs_ref, t, 512, ids)
        contact_ref[t] = -CONTACT_STIFF * once * by_offset(
            table, differences(pairs_ref, t, 512, 127 - ids)
        )
        ids = lax.broadcasted_iota(I32, (128, 256), 0)
        alive = jnp.broadcast_to(broken_ref[pl.ds(t, 1), :], (128, 256)) == 0
        table = jnp.where(alive, differences(bonds_ref, t, 256, ids), 0.0)
        bond_ref[t] = -BOND_DAMP * once * by_offset(
            table, differences(bonds_ref, t, 256, 127 - ids)
        )
        reach = partners(radius[t : t + 1]) + jnp.broadcast_to(radius[t : t + 1], (HALF, 128))
        reach_ref[t] = 1.0 / (reach * reach)
    x8, v8 = state_rows(state_ref)
    force_ref[...] = pair_forces(x8, v8, reach_ref, contact_ref, bond_ref)


def from_sides(even, got_even, got_odd):
    return jnp.where(even, got_odd, got_even), jnp.where(even, got_even, got_odd)


def turn_rows(low, own, high, count):
    return [
        jnp.concatenate(
            [src[3 * f + b : 3 * f + b + 1] for f in range(count) for src in (low, own, high)],
            axis=0,
        )
        for b in range(3)
    ]


def turn_kernel(count, with_cols):
    def kernel(*refs):
        if with_cols:
            got_even_ref, got_odd_ref, own_ref, cols_ref, even_ref, odd_ref, keep_ref = refs
        else:
            got_even_ref, got_odd_ref, own_ref, even_ref, odd_ref, keep_ref = refs
        part = pl.ds(0, 3 * count)
        low, high = from_sides(is_even("ocx"), got_even_ref[part, :], got_odd_ref[part, :])
        down, keep, up = turn_rows(low, own_ref[part, :], high, count)
        even = is_even("ocy")
        send_both(even, up, down, even_ref, odd_ref, 0, 3 * count)
        if with_cols:
            send_both(even, cols_ref[0:4], cols_ref[4:8], even_ref, odd_ref, 12, 4)
        keep_ref[part, :] = keep

    return kernel


def entry_rows(got_even_ref, got_odd_ref, keep_ref, count):
    part = pl.ds(0, 3 * count)
    low, high = from_sides(is_even("ocy"), got_even_ref[part, :], got_odd_ref[part, :])
    keep = keep_ref[part, :]
    return [
        jnp.concatenate(
            [src[3 * f + a : 3 * f + a + 1] for a in range(3) for src in (low, keep, high)], axis=1
        )
        for f in range(count)
    ]


def floe_kernel(
    got_even_ref,
    got_odd_ref,
    keep_ref,
    floe_ref,
    weight_ref,
    table_ref,
    area_ref,
    salt_ref,
    reach_ref,
    contact_ref,
    bond_ref,
    force_ref,
    state_ref,
    props_ref,
    moved_ref,
    even_ref,
    odd_ref,
    own_ref,
):
    samples = entry_rows(got_even_ref, got_odd_ref, keep_ref, 3)
    weight = lanes_row(weight_ref)
    floes = lanes_row(floe_ref)
    table = table_ref[...]
    ids = lax.broadcasted_iota(I32, (8, ENTRIES), 0)
    tile_hit = (ids & 3) == jnp.broadcast_to(floes >> 7, (8, ENTRIES))
    wide = jnp.where(
        ids < 4,
        jnp.broadcast_to(weight * samples[0], (8, ENTRIES)),
        jnp.broadcast_to(weight * samples[1], (8, ENTRIES)),
    )
    drag = join3(dot_nt(split3(jnp.where(tile_hit, wide, 0.0)), table))
    area = area_ref[...]
    radius = tile_rows(props_ref, 0)
    inv_mass = 1.0 / (tile_rows(props_ref, 1) * radius * radius)
    push = TIME_STEP * jnp.concatenate([inv_mass, inv_mass], axis=0)
    x8, v8 = state_rows(state_ref)
    mean = jnp.zeros((8, 128), F32)
    for substep in range(SUBSTEPS):
        if substep == 0:
            force = force_ref[...]
        else:
            force = pair_forces(x8, v8, reach_ref, contact_ref, bond_ref)
        force = force + DRAG_COEF * (drag - area * v8)
        v8 = v8 + push * force
        x8 = x8 + TIME_STEP * v8
        mean = mean + v8 * (1.0 / SUBSTEPS)
    moved_ref[pl.ds(0, 8), :] = x8
    moved_ref[pl.ds(8, 8), :] = v8
    picked = jnp.where(tile_hit, join3(dot_nn(split3(mean), table)), 0.0)
    flux = [
        DRAG_COEF
        * weight
        * (jnp.sum(picked[4 * k : 4 * k + 4], axis=0, keepdims=True) - samples[k])
        for k in range(2)
    ]
    flux = flux + [HEAT_COEF * weight * (FREEZE - samples[2]), salt_ref[...]]
    send_both(
        is_even("ocx"), bucket_rows(flux, 2), bucket_rows(flux, 0), even_ref, odd_ref, 0, 12
    )
    own_ref[pl.ds(0, 12), :] = bucket_rows(flux, 1)


def ocean_kernel(
    ocean_ref,
    x_even_ref,
    x_odd_ref,
    y_even_ref,
    y_odd_ref,
    moved_ref,
    out_ref,
    next_ref,
    low_ref,
    high_ref,
):
    for k in range(4):
        for t in range(TILES):
            next_ref[pl.ds(k, 1), pl.ds(t * 128, 128)] = moved_ref[pl.ds(4 * k + t, 1), :]
    i, j = lax.axis_index("ocx"), lax.axis_index("ocy")
    x_even, y_even = lax.rem(i, 2) == 0, lax.rem(j, 2) == 0
    rows = pl.ds(16, 64)
    low, high = from_sides(x_even, x_even_ref[rows, :], x_odd_ref[rows, :])
    low_ref[...] = jnp.where(i == 0, 0.0, low)
    high_ref[...] = jnp.where(i == lax.axis_size("ocx") - 1, 0.0, high)
    rows = pl.ds(12, 4)
    left, right = from_sides(y_even, y_even_ref[rows, :], y_odd_ref[rows, :])
    left = jnp.where(j == 0, 0.0, left)
    right = jnp.where(j == lax.axis_size("ocy") - 1, 0.0, right)
    turned = jnp.concatenate([left, right], axis=0).T
    sub = lax.broadcasted_iota(I32, (8, 128), 0)
    lane = lax.broadcasted_iota(I32, (8, 128), 1)
    at_low, at_high = sub == 0, sub == 7
    at_left, at_right = lane == 0, lane == 127

    def block(f, l):
        return ocean_ref[pl.ds((f * LEV + l) * 8, 8), :]

    def neighbours(f, l, here):
        k = f * LEV + l
        below = jnp.where(
            at_low, jnp.broadcast_to(low_ref[pl.ds(k, 1), :], (8, 128)), pltpu.roll(here, 1, 0)
        )
        above = jnp.where(
            at_high, jnp.broadcast_to(high_ref[pl.ds(k, 1), :], (8, 128)), pltpu.roll(here, 7, 0)
        )
        edge = turned[l * 8 : l * 8 + 8]
        left = jnp.where(
            at_left, jnp.broadcast_to(edge[:, f : f + 1], (8, 128)), pltpu.roll(here, 1, 1)
        )
        right = jnp.where(
            at_right, jnp.broadcast_to(edge[:, 4 + f : 5 + f], (8, 128)), pltpu.roll(here, 127, 1)
        )
        return below, above, left, right

    grad_x = jnp.zeros((8, 128), F32)
    grad_y = jnp.zeros((8, 128), F32)
    for l in range(LEV):
        here = [block(f, l) for f in range(4)]
        around = [neighbours(f, l, here[f]) for f in range(4)]
        below, above, left, right = zip(*around)
        grad_x = grad_x + (
            (0.5 * HALINE_CONTR) * (above[3] - below[3]) - (0.5 * THERMAL_EXP) * (above[2] - below[2])
        )
        grad_y = grad_y + (
            (0.5 * HALINE_CONTR) * (right[3] - left[3]) - (0.5 * THERMAL_EXP) * (right[2] - left[2])
        )
        for f in range(4):
            side = below[f] + above[f] + left[f] + right[f] - 4.0 * here[f]
            depth = block(f, max(l - 1, 0)) + block(f, min(l + 1, LEV - 1)) - 2.0 * here[f]
            new = here[f] + DIFFUSE_SIDE * side + DIFFUSE_DEPTH * depth
            if f == 0:
                new = new + CORIOLIS * here[1] - PRESSURE_COEF * grad_x
            if f == 1:
                new = new - CORIOLIS * here[0] - PRESSURE_COEF * grad_y
            out_ref[pl.ds((f * LEV + l) * 8, 8), :] = new


def forcing_kernel(got_even_ref, got_odd_ref, keep_ref, cell_ref, ocean_ref, out_ref):
    cells = lanes_row(cell_ref)
    table = one_hot(cells & 127)
    row_hit = lax.broadcasted_iota(I32, (8, ENTRIES), 0) == jnp.broadcast_to(
        cells >> 7, (8, ENTRIES)
    )
    flux = entry_rows(got_even_ref, got_odd_ref, keep_ref, 4)
    spread = jnp.concatenate(
        [jnp.where(row_hit, jnp.broadcast_to(row, (8, ENTRIES)), 0.0) for row in flux], axis=0
    )
    forcing = join3(dot_nt(split3(spread), table))
    out_ref[...] = ocean_ref[...]
    for f in range(4):
        rows = pl.ds(f * LEV * 8, 8)
        out_ref[rows, :] = ocean_ref[rows, :] + forcing[8 * f : 8 * f + 8]


def pairings(nx, ny):
    def both(pair_of):
        return [(i * ny + j, pair_of(i, j)) for i in range(nx) for j in range(ny)]

    def odd_x(i, j):
        if i in (0, nx - 1):
            return i * ny + (j ^ 1)
        return (i + 1 if i % 2 else i - 1) * ny + j

    def odd_y(i, j):
        if j in (0, ny - 1):
            return (i ^ 1) * ny + j
        return i * ny + (j + 1 if j % 2 else j - 1)

    return (
        both(lambda i, j: (i ^ 1) * ny + j),
        both(odd_x),
        both(lambda i, j: i * ny + (j ^ 1)),
        both(odd_y),
    )


def shards(nx, ny):
    x_even, x_odd, y_even, y_odd = pairings(nx, ny)

    def body(
        ocean_state,
        floe_state,
        floe_props,
        contact_pairs,
        bond_ends,
        bond_broken,
        couple_floe,
        couple_weight,
        couple_cell,
    ):
        ocean = ocean_state.reshape(4 * LEV * 8, 128)
        floe = couple_floe.reshape(BUCKETS, 1, 128)
        weight = couple_weight.reshape(BUCKETS, 1, 128)
        cell = couple_cell.reshape(BUCKETS, 1, 128)
        small = shaped(16, 128)
        block = shaped(4 * LEV * 8, 128)
        hbm = pl.BlockSpec(memory_space=pltpu.HBM)
        send_even, send_odd, own, ocean = pl.pallas_call(
            sample_kernel,
            out_shape=(shaped(80, 128), shaped(80, 128), small, block),
            in_specs=[hbm, hbm],
            out_specs=(VMEM_SPEC,) * 4,
            scratch_shapes=[
                pltpu.VMEM((BUCKETS, 1, 128), I32),
                pltpu.VMEM((24, 128), F32),
                pltpu.SemaphoreType.DMA((5,)),
            ],
            compiler_params=GRANT,
        )(in_hbm(ocean), in_hbm(cell))
        ge_x = exchange(send_even, x_even)
        go_x = exchange(send_odd, x_odd)
        cols, table, area, salt = call(
            column_kernel,
            (shaped(8, 128), shaped(128, ENTRIES, dtype=BF16), shaped(8, 128), shaped(1, ENTRIES)),
            ocean,
            floe,
            weight,
            floe_props,
        )
        send_even, send_odd, keep = call(
            turn_kernel(3, True), (small, small, small), ge_x, go_x, own, cols
        )
        ge_y = exchange(send_even, y_even)
        go_y = exchange(send_odd, y_odd)
        square = shaped(TILES, HALF, 128)
        reach, contact, bond, force = call(
            pair_kernel,
            (square, square, square, shaped(8, 128)),
            contact_pairs,
            bond_ends,
            bond_broken,
            floe_props,
            floe_state,
        )
        moved, send_even, send_odd, own = call(
            floe_kernel,
            (small, small, small, small),
            ge_y,
            go_y,
            keep,
            floe,
            weight,
            table,
            area,
            salt,
            reach,
            contact,
            bond,
            force,
            floe_state,
            floe_props,
        )
        he_x = exchange(send_even, x_even)
        ho_x = exchange(send_odd, x_odd)
        send_even, send_odd, keep = call(
            turn_kernel(4, False), (small, small, small), he_x, ho_x, own
        )
        he_y = exchange(send_even, y_even)
        ho_y = exchange(send_odd, y_odd)
        ocean, floe_next = pl.pallas_call(
            ocean_kernel,
            out_shape=(block, shaped(4, 512)),
            in_specs=[VMEM_SPEC] * 6,
            out_specs=(VMEM_SPEC,) * 2,
            scratch_shapes=[pltpu.VMEM((64, 128), F32), pltpu.VMEM((64, 128), F32)],
            compiler_params=GRANT,
        )(ocean, ge_x, go_x, ge_y, go_y, moved)
        ocean_next = call(forcing_kernel, block, he_y, ho_y, keep, cell, ocean)
        return (ocean_next.reshape(ocean_state.shape), floe_next)

    return body


def exchange(data, pairs):
    return lax.ppermute(data, AXES, pairs)


def solution(mesh):
    in_specs = (
        P(None, None, "ocx", "ocy"),
        P(None, ("ocx", "ocy")),
        P(None, ("ocx", "ocy")),
        P(None, ("ocx", "ocy"), None),
        P(None, ("ocx", "ocy"), None),
        P(("ocx", "ocy"), None),
        P(("ocx", "ocy"), None, None),
        P(("ocx", "ocy"), None, None),
        P(("ocx", "ocy"), None, None),
    )
    out_specs = (P(None, None, "ocx", "ocy"), P(None, ("ocx", "ocy")))
    body = shards(mesh.shape["ocx"], mesh.shape["ocy"])
    return jax.shard_map(body, mesh=mesh, in_specs=in_specs, out_specs=out_specs, check_vma=False)
```

```python
import jax
import jax.numpy as jnp
from jax import lax
from jax.experimental import pallas as pl
from jax.experimental.pallas import tpu as pltpu
from jax.sharding import PartitionSpec as P

F32 = jnp.float32
BF16 = jnp.bfloat16
I32 = jnp.int32

TILES = 4
SUBSTEPS = 4
LEV = 16
BUCKETS = 9
ENTRIES = BUCKETS * 128
TIME_STEP = 0.05
CONTACT_STIFF = 2.0
CONTACT_DAMP = 0.2
BOND_DAMP = 0.3
DRAG_COEF = 0.5
HEAT_COEF = 0.3
SALT_COEF = 0.2
FREEZE = -1.8
DIFFUSE_SIDE = 0.15
DIFFUSE_DEPTH = 0.2
CORIOLIS = 0.3
PRESSURE_COEF = 0.1
THERMAL_EXP = 0.2
HALINE_CONTR = 0.8
AXES = ("ocx", "ocy")
VMEM_SPEC = pl.BlockSpec(memory_space=pltpu.VMEM)
GRANT = pltpu.CompilerParams(vmem_limit_bytes=8 << 20)


def call(kernel, outs, *args, cost=0):
    return pl.pallas_call(
        kernel,
        out_shape=outs,
        in_specs=[VMEM_SPEC] * len(args),
        out_specs=jax.tree.map(lambda _: VMEM_SPEC, outs),
        cost_estimate=pl.CostEstimate(flops=cost, bytes_accessed=1 << 16, transcendentals=0),
        compiler_params=GRANT,
    )(*args)


def in_hbm(x):
    return pltpu.with_memory_space_constraint(x, pltpu.HBM)


def shaped(*shape, dtype=F32):
    return jax.ShapeDtypeStruct(shape, dtype)


def split3(x):
    hi = x.astype(BF16).astype(F32)
    rest = x - hi
    mid = rest.astype(BF16).astype(F32)
    return jnp.concatenate([hi, mid, rest - mid], axis=0).astype(BF16)


def join3(y):
    n = y.shape[0] // 3
    return y[:n] + y[n : 2 * n] + y[2 * n :]


def dot_nn(a, b):
    return lax.dot_general(a, b, (((1,), (0,)), ((), ())), preferred_element_type=F32)


def dot_nt(a, b):
    return lax.dot_general(a, b, (((1,), (1,)), ((), ())), preferred_element_type=F32)


def lanes_row(ref):
    return jnp.concatenate([ref[m] for m in range(BUCKETS)], axis=1)


def one_hot(row):
    n = row.shape[1]
    ids = lax.broadcasted_iota(I32, (128, n), 0)
    return jnp.where(ids == jnp.broadcast_to(row, (128, n)), 1.0, 0.0).astype(BF16)


def is_even(axis):
    return lax.rem(lax.axis_index(axis), 2) == 0


def send_both(even, toward_plus, toward_minus, even_ref, odd_ref, row, rows):
    even_ref[pl.ds(row, rows), :] = jnp.where(even, toward_plus, toward_minus)
    odd_ref[pl.ds(row, rows), :] = jnp.where(even, toward_minus, toward_plus)


def bucket_rows(fields, a):
    rows = [f[:, (3 * a + b) * 128 : (3 * a + b + 1) * 128] for f in fields for b in range(3)]
    return jnp.concatenate(rows, axis=0)


def sample_kernel(ocean_hbm, cell_hbm, even_ref, odd_ref, own_ref, cell_ref, surface_ref, sems):
    copies = [pltpu.make_async_copy(cell_hbm, cell_ref, sems.at[0])]
    for f in range(3):
        copies.append(
            pltpu.make_async_copy(
                ocean_hbm.at[pl.ds(f * LEV * 8, 8), :],
                surface_ref.at[pl.ds(f * 8, 8), :],
                sems.at[1 + f],
            )
        )
    for copy in copies:
        copy.start()
    for copy in copies:
        copy.wait()
    even = is_even("ocx")
    cells = lanes_row(cell_ref)
    table = one_hot(cells & 127)
    picked = join3(dot_nn(split3(surface_ref[...]), table))
    row_hit = lax.broadcasted_iota(I32, (8, ENTRIES), 0) == jnp.broadcast_to(
        cells >> 7, (8, ENTRIES)
    )
    fields = [
        jnp.sum(jnp.where(row_hit, picked[8 * f : 8 * f + 8], 0.0), axis=0, keepdims=True)
        for f in range(3)
    ]
    send_both(even, bucket_rows(fields, 2), bucket_rows(fields, 0), even_ref, odd_ref, 0, 9)
    own_ref[pl.ds(0, 9), :] = bucket_rows(fields, 1)


def tile_mask(floes):
    ids = lax.broadcasted_iota(I32, (8, ENTRIES), 0)
    return (ids >> 1) == jnp.broadcast_to(floes >> 7, (8, ENTRIES)), (ids & 1) == 0


def column_kernel(
    ocean_ref,
    floe_ref,
    weight_ref,
    props_ref,
    cols_ref,
    table_ref,
    area_ref,
    salt_ref,
    even_ref,
    odd_ref,
):
    first = ocean_ref[pl.ds(0, 64, stride=8), :]
    last = ocean_ref[pl.ds(7, 64, stride=8), :]
    send_both(is_even("ocx"), last, first, even_ref, odd_ref, 0, 64)
    for f in range(4):
        turned = ocean_ref[pl.ds(f * 128, 128), :].T
        cols_ref[pl.ds(f, 1), :] = turned[127:128]
        cols_ref[pl.ds(4 + f, 1), :] = turned[0:1]
    floes = lanes_row(floe_ref)
    weight = lanes_row(weight_ref)
    table = one_hot(floes & 127)
    table_ref[...] = table
    tile_hit, first_row = tile_mask(floes)
    spread = jnp.where(tile_hit, jnp.broadcast_to(weight, (8, ENTRIES)), 0.0)
    area_ref[...] = join3(dot_nt(split3(spread), table))
    thick = jnp.concatenate(
        [
            jnp.broadcast_to(props_ref[pl.ds(1, 1), pl.ds(t * 128, 128)], (2, 128))
            for t in range(TILES)
        ],
        axis=0,
    )
    picked = join3(dot_nn(split3(thick), table))
    chosen = jnp.sum(jnp.where(tile_hit & first_row, picked, 0.0), axis=0, keepdims=True)
    salt_ref[...] = SALT_COEF * weight * chosen


def pair_force(t, place, speed, reach_ref, contact_ref, bond_ref):
    lean = (CONTACT_DAMP / CONTACT_STIFF) * speed - place

    def across(rows, k):
        return jnp.broadcast_to(rows[k : k + 1], (128, 128)).T

    columns = [across(rows, k) for rows in (place, lean) for k in range(2)]
    step = 32
    totals = [jnp.zeros((8, 128), F32)] * 2
    for lo in range(0, 128, step):
        part = pl.ds(lo, step)
        dx, dy, wx, wy = [
            column[lo : lo + step] - jnp.broadcast_to(rows[k : k + 1], (step, 128))
            for column, (rows, k) in zip(
                columns, ((place, 0), (place, 1), (lean, 0), (lean, 1))
            )
        ]
        depth = jnp.maximum(1.0 - (dx * dx + dy * dy) * reach_ref[t, part, :], 0.0)
        stiff = depth * contact_ref[t, part, :]
        totals = [
            total + jnp.sum((stiff * w).reshape(step // 8, 8, 128), axis=0)
            for total, w in zip(totals, (wx, wy))
        ]
    contact = jnp.concatenate([jnp.sum(x, axis=0, keepdims=True) for x in totals], axis=0)
    padded = jnp.concatenate([speed, jnp.zeros((6, 128), F32)], axis=0)
    return contact - BOND_DAMP * join3(dot_nn(split3(padded), bond_ref[t]))[:2]


def tile_state(state_ref, t):
    lanes = pl.ds(t * 128, 128)
    return state_ref[pl.ds(0, 2), lanes], state_ref[pl.ds(2, 2), lanes]


def pair_kernel(
    pairs_ref, bonds_ref, broken_ref, props_ref, state_ref, reach_ref, contact_ref, bond_ref, force_ref
):
    def differences(ref, t, n):
        ids = lax.broadcasted_iota(I32, (128, n), 0)
        first = jnp.broadcast_to(ref[0, pl.ds(t, 1), :], (128, n))
        second = jnp.broadcast_to(ref[1, pl.ds(t, 1), :], (128, n))
        return jnp.where(ids == second, 1.0, 0.0) - jnp.where(ids == first, 1.0, 0.0)

    for t in range(TILES):
        slots = differences(pairs_ref, t, 512).astype(BF16)
        contact_ref[t] = -CONTACT_STIFF * dot_nt(slots, slots)
        alive = jnp.broadcast_to(broken_ref[pl.ds(t, 1), :], (128, 256)) == 0
        ends = jnp.where(alive, differences(bonds_ref, t, 256), 0.0).astype(BF16)
        bond_ref[t] = dot_nt(ends, ends).astype(BF16)
        radius = jnp.broadcast_to(props_ref[pl.ds(0, 1), pl.ds(t * 128, 128)], (128, 128))
        reach = radius + radius.T
        reach_ref[t] = 1.0 / (reach * reach)
    for t in range(TILES):
        place, speed = tile_state(state_ref, t)
        force_ref[pl.ds(2 * t, 2), :] = pair_force(
            t, place, speed, reach_ref, contact_ref, bond_ref
        )


def from_sides(even, got_even, got_odd):
    return jnp.where(even, got_odd, got_even), jnp.where(even, got_even, got_odd)


def turn_rows(low, own, high, count):
    return [
        jnp.concatenate(
            [src[3 * f + b : 3 * f + b + 1] for f in range(count) for src in (low, own, high)],
            axis=0,
        )
        for b in range(3)
    ]


def turn_kernel(count, with_cols):
    def kernel(*refs):
        if with_cols:
            got_even_ref, got_odd_ref, own_ref, cols_ref, even_ref, odd_ref, keep_ref = refs
        else:
            got_even_ref, got_odd_ref, own_ref, even_ref, odd_ref, keep_ref = refs
        part = pl.ds(0, 3 * count)
        low, high = from_sides(is_even("ocx"), got_even_ref[part, :], got_odd_ref[part, :])
        down, keep, up = turn_rows(low, own_ref[part, :], high, count)
        even = is_even("ocy")
        send_both(even, up, down, even_ref, odd_ref, 0, 3 * count)
        if with_cols:
            send_both(even, cols_ref[0:4], cols_ref[4:8], even_ref, odd_ref, 12, 4)
        keep_ref[part, :] = keep

    return kernel


def entry_rows(got_even_ref, got_odd_ref, keep_ref, count):
    part = pl.ds(0, 3 * count)
    low, high = from_sides(is_even("ocy"), got_even_ref[part, :], got_odd_ref[part, :])
    keep = keep_ref[part, :]
    return [
        jnp.concatenate(
            [src[3 * f + a : 3 * f + a + 1] for a in range(3) for src in (low, keep, high)], axis=1
        )
        for f in range(count)
    ]


def floe_kernel(
    got_even_ref,
    got_odd_ref,
    keep_ref,
    floe_ref,
    weight_ref,
    table_ref,
    area_ref,
    salt_ref,
    reach_ref,
    contact_ref,
    bond_ref,
    force_ref,
    state_ref,
    props_ref,
    moved_ref,
    even_ref,
    odd_ref,
    own_ref,
):
    samples = entry_rows(got_even_ref, got_odd_ref, keep_ref, 3)
    weight = lanes_row(weight_ref)
    table = table_ref[...]
    tile_hit, first_row = tile_mask(lanes_row(floe_ref))
    wide = jnp.where(
        first_row,
        jnp.broadcast_to(weight * samples[0], (8, ENTRIES)),
        jnp.broadcast_to(weight * samples[1], (8, ENTRIES)),
    )
    drags = join3(dot_nt(split3(jnp.where(tile_hit, wide, 0.0)), table))
    area_rows = area_ref[...]
    first_force = force_ref[...]
    tiles = range(TILES)
    states = [tile_state(state_ref, t) for t in tiles]
    means = [jnp.zeros((2, 128), F32)] * TILES
    push = []
    for t in tiles:
        lanes = pl.ds(t * 128, 128)
        radius, thick = props_ref[pl.ds(0, 1), lanes], props_ref[pl.ds(1, 1), lanes]
        push.append(TIME_STEP * (1.0 / (thick * radius * radius)))
    for substep in range(SUBSTEPS):
        for t in tiles:
            place, speed = states[t]
            rows = slice(2 * t, 2 * t + 2)
            if substep == 0:
                force = first_force[rows]
            else:
                force = pair_force(t, place, speed, reach_ref, contact_ref, bond_ref)
            force = force + DRAG_COEF * (drags[rows] - area_rows[rows] * speed)
            speed = speed + push[t] * force
            place = place + TIME_STEP * speed
            means[t] = means[t] + speed * (1.0 / SUBSTEPS)
            states[t] = (place, speed)
    for t in tiles:
        moved_ref[pl.ds(4 * t, 2), :] = states[t][0]
        moved_ref[pl.ds(4 * t + 2, 2), :] = states[t][1]
    picked = jnp.where(
        tile_hit, join3(dot_nn(split3(jnp.concatenate(means, axis=0)), table)), 0.0
    )
    speeds = [jnp.where(first_row, picked, 0.0), jnp.where(first_row, 0.0, picked)]
    flux = [
        DRAG_COEF * weight * (jnp.sum(speeds[k], axis=0, keepdims=True) - samples[k])
        for k in range(2)
    ]
    flux = flux + [HEAT_COEF * weight * (FREEZE - samples[2]), salt_ref[...]]
    send_both(
        is_even("ocx"), bucket_rows(flux, 2), bucket_rows(flux, 0), even_ref, odd_ref, 0, 12
    )
    own_ref[pl.ds(0, 12), :] = bucket_rows(flux, 1)


def ocean_kernel(
    ocean_ref,
    x_even_ref,
    x_odd_ref,
    y_even_ref,
    y_odd_ref,
    moved_ref,
    out_ref,
    top_ref,
    next_ref,
    low_ref,
    high_ref,
):
    for t in range(TILES):
        next_ref[:, pl.ds(t * 128, 128)] = moved_ref[pl.ds(4 * t, 4), :]
    i, j = lax.axis_index("ocx"), lax.axis_index("ocy")
    x_even, y_even = lax.rem(i, 2) == 0, lax.rem(j, 2) == 0
    low, high = from_sides(x_even, x_even_ref[...], x_odd_ref[...])
    low_ref[...] = jnp.where(i == 0, 0.0, low)
    high_ref[...] = jnp.where(i == lax.axis_size("ocx") - 1, 0.0, high)
    rows = pl.ds(12, 4)
    left, right = from_sides(y_even, y_even_ref[rows, :], y_odd_ref[rows, :])
    left = jnp.where(j == 0, 0.0, left)
    right = jnp.where(j == lax.axis_size("ocy") - 1, 0.0, right)
    turned = jnp.concatenate([left, right], axis=0).T
    sub = lax.broadcasted_iota(I32, (8, 128), 0)
    lane = lax.broadcasted_iota(I32, (8, 128), 1)
    at_low, at_high = sub == 0, sub == 7
    at_left, at_right = lane == 0, lane == 127

    def block(f, l):
        return ocean_ref[pl.ds((f * LEV + l) * 8, 8), :]

    def neighbours(f, l, here):
        k = f * LEV + l
        below = jnp.where(
            at_low, jnp.broadcast_to(low_ref[pl.ds(k, 1), :], (8, 128)), pltpu.roll(here, 1, 0)
        )
        above = jnp.where(
            at_high, jnp.broadcast_to(high_ref[pl.ds(k, 1), :], (8, 128)), pltpu.roll(here, 7, 0)
        )
        edge = turned[l * 8 : l * 8 + 8]
        left = jnp.where(
            at_left, jnp.broadcast_to(edge[:, f : f + 1], (8, 128)), pltpu.roll(here, 1, 1)
        )
        right = jnp.where(
            at_right, jnp.broadcast_to(edge[:, 4 + f : 5 + f], (8, 128)), pltpu.roll(here, 127, 1)
        )
        return below, above, left, right

    grad_x = jnp.zeros((8, 128), F32)
    grad_y = jnp.zeros((8, 128), F32)
    for l in range(LEV):
        here = [block(f, l) for f in range(4)]
        around = [neighbours(f, l, here[f]) for f in range(4)]
        below, above, left, right = zip(*around)
        grad_x = grad_x + (
            (0.5 * HALINE_CONTR) * (above[3] - below[3]) - (0.5 * THERMAL_EXP) * (above[2] - below[2])
        )
        grad_y = grad_y + (
            (0.5 * HALINE_CONTR) * (right[3] - left[3]) - (0.5 * THERMAL_EXP) * (right[2] - left[2])
        )
        for f in range(4):
            side = below[f] + above[f] + left[f] + right[f] - 4.0 * here[f]
            depth = block(f, max(l - 1, 0)) + block(f, min(l + 1, LEV - 1)) - 2.0 * here[f]
            new = here[f] + DIFFUSE_SIDE * side + DIFFUSE_DEPTH * depth
            if f == 0:
                new = new + CORIOLIS * here[1] - PRESSURE_COEF * grad_x
            if f == 1:
                new = new - CORIOLIS * here[0] - PRESSURE_COEF * grad_y
            if l == 0:
                top_ref[pl.ds(f * 8, 8), :] = new
            out_ref[pl.ds((f * LEV + l) * 8, 8), :] = new


def forcing_kernel(
    got_even_ref, got_odd_ref, keep_ref, cell_ref, top_ref, ocean_hbm, out_hbm, sum_ref, sems
):
    del ocean_hbm
    cells = lanes_row(cell_ref)
    table = one_hot(cells & 127)
    row_hit = lax.broadcasted_iota(I32, (8, ENTRIES), 0) == jnp.broadcast_to(
        cells >> 7, (8, ENTRIES)
    )
    flux = entry_rows(got_even_ref, got_odd_ref, keep_ref, 4)
    spread = jnp.concatenate(
        [jnp.where(row_hit, jnp.broadcast_to(row, (8, ENTRIES)), 0.0) for row in flux], axis=0
    )
    forcing = join3(dot_nt(split3(spread), table))
    sum_ref[...] = top_ref[...] + forcing
    copies = [
        pltpu.make_async_copy(
            sum_ref.at[pl.ds(f * 8, 8), :], out_hbm.at[pl.ds(f * LEV * 8, 8), :], sems.at[f]
        )
        for f in range(4)
    ]
    for copy in copies:
        copy.start()
    for copy in copies:
        copy.wait()


def pairings(nx, ny):
    def both(pair_of):
        return [(i * ny + j, pair_of(i, j)) for i in range(nx) for j in range(ny)]

    def odd_x(i, j):
        if i in (0, nx - 1):
            return i * ny + (j ^ 4)
        return (i + 1 if i % 2 else i - 1) * ny + j

    def odd_y(i, j):
        if j in (0, ny - 1):
            return (i ^ 1) * ny + j
        return i * ny + (j + 1 if j % 2 else j - 1)

    return (
        both(lambda i, j: (i ^ 1) * ny + j),
        both(odd_x),
        both(lambda i, j: i * ny + (j ^ 1)),
        both(odd_y),
    )


def shards(nx, ny):
    x_even, x_odd, y_even, y_odd = pairings(nx, ny)

    def body(
        ocean_state,
        floe_state,
        floe_props,
        contact_pairs,
        bond_ends,
        bond_broken,
        couple_floe,
        couple_weight,
        couple_cell,
    ):
        ocean = ocean_state.reshape(4 * LEV * 8, 128)
        floe = couple_floe.reshape(BUCKETS, 1, 128)
        weight = couple_weight.reshape(BUCKETS, 1, 128)
        cell = couple_cell.reshape(BUCKETS, 1, 128)
        small = shaped(16, 128)
        block = shaped(4 * LEV * 8, 128)
        hbm = pl.BlockSpec(memory_space=pltpu.HBM)
        send_even, send_odd, own = pl.pallas_call(
            sample_kernel,
            out_shape=(small, small, small),
            in_specs=[hbm, hbm],
            out_specs=(VMEM_SPEC,) * 3,
            scratch_shapes=[
                pltpu.VMEM((BUCKETS, 1, 128), I32),
                pltpu.VMEM((24, 128), F32),
                pltpu.SemaphoreType.DMA((4,)),
            ],
            compiler_params=GRANT,
        )(in_hbm(ocean), in_hbm(cell))
        ge_x = exchange(send_even, x_even)
        go_x = exchange(send_odd, x_odd)
        cols, table, area, salt, edge_even, edge_odd = call(
            column_kernel,
            (
                shaped(8, 128),
                shaped(128, ENTRIES, dtype=BF16),
                shaped(8, 128),
                shaped(1, ENTRIES),
                shaped(64, 128),
                shaped(64, 128),
            ),
            ocean,
            floe,
            weight,
            floe_props,
        )
        send_even, send_odd, keep = call(
            turn_kernel(3, True), (small, small, small), ge_x, go_x, own, cols
        )
        ge_y = exchange(send_even, y_even)
        go_y = exchange(send_odd, y_odd)
        edge_even = exchange(edge_even, x_even)
        edge_odd = exchange(edge_odd, x_odd)
        square = shaped(TILES, 128, 128)
        reach, contact, bond, force = call(
            pair_kernel,
            (square, square, shaped(TILES, 128, 128, dtype=BF16), shaped(8, 128)),
            contact_pairs,
            bond_ends,
            bond_broken,
            floe_props,
            floe_state,
        )
        moved, send_even, send_odd, own = call(
            floe_kernel,
            (small, small, small, small),
            ge_y,
            go_y,
            keep,
            floe,
            weight,
            table,
            area,
            salt,
            reach,
            contact,
            bond,
            force,
            floe_state,
            floe_props,
        )
        he_x = exchange(send_even, x_even)
        ho_x = exchange(send_odd, x_odd)
        send_even, send_odd, keep = call(
            turn_kernel(4, False), (small, small, small), he_x, ho_x, own
        )
        he_y = exchange(send_even, y_even)
        ho_y = exchange(send_odd, y_odd)
        ocean, top, floe_next = pl.pallas_call(
            ocean_kernel,
            out_shape=(block, shaped(32, 128), shaped(4, 512)),
            in_specs=[VMEM_SPEC] * 6,
            out_specs=(VMEM_SPEC,) * 3,
            scratch_shapes=[pltpu.VMEM((64, 128), F32), pltpu.VMEM((64, 128), F32)],
            compiler_params=GRANT,
        )(ocean, edge_even, edge_odd, ge_y, go_y, moved)
        ocean_next = pl.pallas_call(
            forcing_kernel,
            out_shape=block,
            in_specs=[VMEM_SPEC] * 5 + [hbm],
            out_specs=hbm,
            scratch_shapes=[pltpu.VMEM((32, 128), F32), pltpu.SemaphoreType.DMA((4,))],
            input_output_aliases={5: 0},
            compiler_params=GRANT,
        )(he_y, ho_y, keep, cell, top, in_hbm(ocean))
        return (ocean_next.reshape(ocean_state.shape), floe_next)

    return body


def exchange(data, pairs):
    return lax.ppermute(data, AXES, pairs)


def solution(mesh):
    in_specs = (
        P(None, None, "ocx", "ocy"),
        P(None, ("ocx", "ocy")),
        P(None, ("ocx", "ocy")),
        P(None, ("ocx", "ocy"), None),
        P(None, ("ocx", "ocy"), None),
        P(("ocx", "ocy"), None),
        P(("ocx", "ocy"), None, None),
        P(("ocx", "ocy"), None, None),
        P(("ocx", "ocy"), None, None),
    )
    out_specs = (P(None, None, "ocx", "ocy"), P(None, ("ocx", "ocy")))
    body = shards(mesh.shape["ocx"], mesh.shape["ocy"])
    return jax.shard_map(body, mesh=mesh, in_specs=in_specs, out_specs=out_specs, check_vma=False)
```
